512 devices in a mesh: dp: 8 (over z_lo, core), seq: 64 (over x, y, z_hi).
Axes of the slice: x: 4, y: 8, z: 8 (z_hi: 2, z_lo: 4; z = z_hi * 4 + z_lo), core: 2. Of those that a mesh axis runs over, the one named last changes fastest.
Arguments:
- queries: bfloat16 [8, 8192, 1024], P('dp', 'seq'), may hold values from -6 to 6
- keys: bfloat16 [8, 8192, 1024], P('dp', 'seq'), may hold values from -6 to 6
- values: bfloat16 [8, 8192, 1024], P('dp', 'seq'), may hold values from -6 to 6
- grad_out: bfloat16 [8, 8192, 1024], P('dp', 'seq'), may hold values from -6 to 6
- mem_keys: bfloat16 [64, 512, 1024], P('dp', 'seq'), may hold values from -6 to 6
- mem_values: bfloat16 [64, 512, 1024], P('dp', 'seq'), may hold values from -6 to 6
- seq_lengths: int32 [8], replicated, may hold values from 256 to 8192, as said below
- mem_counts: int32 [8], replicated, may hold values from 1 to 4, as said below
- block_lists: int32 [8, 4], replicated, may hold values from 0 to 63, as said below
- block_slots: int32 [64], replicated, may hold values from 0 to 63, each once
Outputs:
- grad_queries: bfloat16 [8, 8192, 1024], P('dp', 'seq')
- grad_keys: bfloat16 [8, 8192, 1024], P('dp', 'seq')
- grad_values: bfloat16 [8, 8192, 1024], P('dp', 'seq')
The draws below stay inside these ranges and needn't reach their ends.
Inputs may be any that keep to these rules, and one draw needn't show every extreme that they name: `seq_lengths`: some user has all 8192 events. `mem_counts`: some user attends to all 4 listed blocks. `block_lists`: the 4 ids of one user are distinct. `block_slots`: A permutation of the block ids.
All inputs are finite; a program needn't handle non-finite values.
Results may differ from the reference program's by a relative error of at most 0.0063.
Values may be sent and summed in bfloat16 or wider, within the bound.
A program may use at most 128 MiB of HBM per device.

```python
import math
import jax
import jax.numpy as jnp
from jax import lax

D = 1024
H = 8
WINDOW = 512
BLK = 512
MB = 4
TOK_DEV = 128
USERS = 8
SEQLEN = 8192
NBLK = 64


def joint_rows(key):
    query_draw = jnp.clip(jax.random.normal(jax.random.fold_in(key, 11), (USERS, SEQLEN, D), jnp.float32), -6.0, 6.0)
    key_draw = jnp.clip(jax.random.normal(jax.random.fold_in(key, 12), (USERS, SEQLEN, D), jnp.float32), -6.0, 6.0)
    return (query_draw, key_draw)


def draw_queries(key, part):
    return joint_rows(key)[0].astype(jnp.bfloat16)


def draw_keys(key, part):
    return joint_rows(key)[1].astype(jnp.bfloat16)


def draw_seq_lengths(key, part):
    drawn = jax.random.randint(jax.random.fold_in(key, 21), (USERS,), 2 * TOK_DEV, SEQLEN + 1, jnp.int32)
    chosen = jax.random.randint(jax.random.fold_in(key, 22), (), 0, USERS, jnp.int32)
    return jnp.where(jnp.arange(USERS, dtype=jnp.int32) == chosen, SEQLEN, drawn).astype(jnp.int32)


def draw_mem_counts(key, part):
    drawn = jax.random.randint(jax.random.fold_in(key, 31), (USERS,), 1, MB + 1, jnp.int32)
    chosen = jax.random.randint(jax.random.fold_in(key, 32), (), 0, USERS, jnp.int32)
    return jnp.where(jnp.arange(USERS, dtype=jnp.int32) == chosen, MB, drawn).astype(jnp.int32)


def draw_block_lists(key, part):
    user_keys = jax.random.split(jax.random.fold_in(key, 41), USERS)

    def listing(user_key):
        return jax.random.permutation(user_key, NBLK)[:MB]
    return jax.vmap(listing)(user_keys).astype(jnp.int32)


def block_levels(rng, extent, pieces, low, largest):
    loudness, own = 1.0, jax.random.fold_in(rng, 6)
    for position, blocks in pieces:
        draws = jnp.exp(jax.random.uniform(jax.random.fold_in(own, position), (blocks,), jnp.float32, low / len(pieces), largest / len(pieces)))
        loudness = loudness * jnp.repeat(draws, extent[position] // blocks).reshape([-1 if axis == position else 1 for axis in range(len(extent))])
    return loudness


def scatter_about(key, dims, scale, most, cuts=(), held_as=jnp.bfloat16):
    result = scale * jax.random.normal(key, dims, jnp.float32)
    if cuts:
        result = result * block_levels(key, dims, cuts, -0.22, 0.18)
    return jnp.clip(result, -most, most).astype(held_as)


def setup_inputs(seed: int = 0) -> dict:
    arg_keys = jax.random.split(jax.random.key(seed), 11)
    return {
        "queries": draw_queries(jax.random.fold_in(arg_keys[10], 71), 0),
        "keys": draw_keys(jax.random.fold_in(arg_keys[10], 71), 0),
        "values": scatter_about(arg_keys[2], (USERS, SEQLEN, D), 1.0, 6.0, ((0, 8), (1, 64))),
        "grad_out": scatter_about(arg_keys[3], (USERS, SEQLEN, D), 1.0, 6.0, ((0, 8), (1, 64))),
        "mem_keys": scatter_about(arg_keys[4], (NBLK, BLK, D), 1.0, 6.0, ((0, 8), (1, 64))),
        "mem_values": scatter_about(arg_keys[5], (NBLK, BLK, D), 1.0, 6.0, ((0, 8), (1, 64))),
        "seq_lengths": draw_seq_lengths(jax.random.fold_in(arg_keys[10], 71), 0),
        "mem_counts": draw_mem_counts(jax.random.fold_in(arg_keys[10], 71), 0),
        "block_lists": draw_block_lists(jax.random.fold_in(arg_keys[10], 71), 0),
        "block_slots": jax.random.permutation(arg_keys[9], NBLK).astype(jnp.int32),
    }


def head_terms(query_h, key_h, value_h, grad_h, memk_h, memv_h, allow_window, allow_memory):
    scaling = 1.0 / math.sqrt(query_h.shape[1])
    score_w = jnp.dot(query_h, key_h.T, preferred_element_type=jnp.float32) * scaling
    score_m = jnp.dot(query_h, memk_h.T, preferred_element_type=jnp.float32) * scaling
    score_w = jnp.where(allow_window, score_w, -1e+30)
    score_m = jnp.where(allow_memory, score_m, -1e+30)
    row_top = jnp.maximum(lax.optimization_barrier(jnp.max(score_w, axis=1)), lax.optimization_barrier(jnp.max(score_m, axis=1)))
    expo_w = jnp.exp(score_w - row_top[:, None])
    expo_m = jnp.exp(score_m - row_top[:, None])
    totals = lax.optimization_barrier(jnp.sum(expo_w, axis=1)) + lax.optimization_barrier(jnp.sum(expo_m, axis=1))
    prob_w = expo_w / totals[:, None]
    prob_m = expo_m / totals[:, None]
    half_w = prob_w.astype(jnp.bfloat16)
    half_m = prob_m.astype(jnp.bfloat16)
    output = jnp.dot(half_w, value_h, preferred_element_type=jnp.float32) + jnp.dot(half_m, memv_h, preferred_element_type=jnp.float32)
    deltas = lax.optimization_barrier(jnp.sum(grad_h.astype(jnp.float32) * output, axis=1))
    dprob_w = jnp.dot(grad_h, value_h.T, preferred_element_type=jnp.float32)
    dprob_m = jnp.dot(grad_h, memv_h.T, preferred_element_type=jnp.float32)
    dscore_w = (prob_w * (dprob_w - deltas[:, None])).astype(jnp.bfloat16)
    dscore_m = (prob_m * (dprob_m - deltas[:, None])).astype(jnp.bfloat16)
    grad_query = (jnp.dot(dscore_w, key_h, preferred_element_type=jnp.float32) + jnp.dot(dscore_m, memk_h, preferred_element_type=jnp.float32)) * scaling
    grad_key = jnp.dot(dscore_w.T, query_h, preferred_element_type=jnp.float32) * scaling
    grad_value = jnp.dot(half_w.T, grad_h, preferred_element_type=jnp.float32)
    return (grad_query, grad_key, grad_value)

def combine_heads(stacked):
    return jnp.transpose(stacked, (1, 0, 2)).reshape(stacked.shape[1], stacked.shape[0] * stacked.shape[2])

def all_heads(query_rows, key_rows, value_rows, grad_rows, memk_rows, memv_rows, allow_window, allow_memory):
    width = query_rows.shape[1] // H

    def per_head(index):

        def column_slice(tensor):
            return lax.dynamic_slice_in_dim(tensor, index * width, width, 1)
        return head_terms(column_slice(query_rows), column_slice(key_rows), column_slice(value_rows), column_slice(grad_rows), column_slice(memk_rows), column_slice(memv_rows), allow_window, allow_memory)
    grad_query, grad_key, grad_value = lax.map(per_head, jnp.arange(H, dtype=jnp.int32))
    return (combine_heads(grad_query), combine_heads(grad_key), combine_heads(grad_value))

def reference(queries, keys, values, grad_out, mem_keys, mem_values, seq_lengths, mem_counts, block_lists, block_slots):
    reach = WINDOW // TOK_DEV
    padding = reach * TOK_DEV
    nblocks = SEQLEN // TOK_DEV

    def one_user(user):
        length = seq_lengths[user]
        count = mem_counts[user]
        slots = block_slots[block_lists[user]]
        memk_rows = mem_keys[slots].reshape(MB * BLK, D)
        memv_rows = mem_values[slots].reshape(MB * BLK, D)
        zeros_pad = jnp.zeros((padding, D), jnp.bfloat16)
        key_pad = jnp.concatenate([zeros_pad, keys[user]], axis=0)
        value_pad = jnp.concatenate([zeros_pad, values[user]], axis=0)
        event_pos = jnp.arange(SEQLEN, dtype=jnp.int32)
        masked = grad_out[user] * (event_pos < length)[:, None].astype(jnp.bfloat16)
        allow_memory = (jnp.arange(MB * BLK, dtype=jnp.int32) // BLK < count)[None, :]

        def one_block(block):
            start = (block * TOK_DEV).astype(jnp.int32)
            query_rows = lax.dynamic_slice_in_dim(queries[user], start, TOK_DEV, 0)
            grad_rows = lax.dynamic_slice_in_dim(masked, start, TOK_DEV, 0)
            key_rows = lax.dynamic_slice_in_dim(key_pad, start, padding + TOK_DEV, 0)
            value_rows = lax.dynamic_slice_in_dim(value_pad, start, padding + TOK_DEV, 0)
            query_pos = start + jnp.arange(TOK_DEV, dtype=jnp.int32)
            key_pos = start - padding + jnp.arange(padding + TOK_DEV, dtype=jnp.int32)
            allow_window = (key_pos[None, :] <= query_pos[:, None]) & (query_pos[:, None] - key_pos[None, :] < WINDOW) & (key_pos[None, :] >= 0) & ((key_pos[None, :] < length) | (key_pos[None, :] == query_pos[:, None]))
            return all_heads(query_rows, key_rows, value_rows, grad_rows, memk_rows, memv_rows, allow_window, allow_memory)
        grad_query, grad_key, grad_value = lax.map(one_block, jnp.arange(nblocks, dtype=jnp.int32))
        key_total = jnp.zeros((SEQLEN + padding, D), jnp.float32)
        value_total = jnp.zeros((SEQLEN + padding, D), jnp.float32)
        for offset in range(reach + 1):
            key_total = key_total.at[offset * TOK_DEV:offset * TOK_DEV + SEQLEN].add(grad_key[:, offset * TOK_DEV:(offset + 1) * TOK_DEV].reshape(SEQLEN, D))
            value_total = value_total.at[offset * TOK_DEV:offset * TOK_DEV + SEQLEN].add(grad_value[:, offset * TOK_DEV:(offset + 1) * TOK_DEV].reshape(SEQLEN, D))
        return (grad_query.reshape(SEQLEN, D).astype(jnp.bfloat16), key_total[padding:].astype(jnp.bfloat16), value_total[padding:].astype(jnp.bfloat16))
    grad_queries, grad_keys, grad_values = lax.map(one_user, jnp.arange(USERS, dtype=jnp.int32))
    return (grad_queries, grad_keys, grad_values)
```

```python
import functools
import math

import jax
import jax.numpy as jnp
from jax import lax
from jax.experimental import pallas as pl
from jax.experimental.pallas import tpu as pltpu
from jax.sharding import PartitionSpec as P

MESH = pl.DeviceIdType.MESH
ANY = pl.BlockSpec(memory_space=pl.ANY)
VMEM = pl.BlockSpec(memory_space=pltpu.VMEM)
SMEM = pl.BlockSpec(memory_space=pltpu.SMEM)
H = 8
WINDOW = 512
BLK = 512
NX, NY, NZ, ZL = 4, 8, 2, 4
ROWS, HEAD = 128, 128
PAIR = NZ * ROWS
GROUP = [(a, b) for a in range(NX) for b in range(NZ)]
LOG2E = math.log2(math.e)
BARRED = -1e30


def place():
    dp, seq = lax.axis_index("dp"), lax.axis_index("seq")
    return dp // 2, dp % 2, seq // (NY * NZ), (seq // NZ) % NY, seq % NZ


def device(zl, core, x, y, zh):
    return (zl * 2 + core, (x * NY + y) * NZ + zh)


def greet(partners):
    barrier = pltpu.get_barrier_semaphore()
    for partner in partners:
        pl.semaphore_signal(barrier, inc=1, device_id=partner, device_id_type=MESH)
    pl.semaphore_wait(barrier, len(partners))


def remote(src, dst, send, recv, to):
    return pltpu.make_async_remote_copy(
        src_ref=src, dst_ref=dst, send_sem=send, recv_sem=recv, device_id=to, device_id_type=MESH
    )


def columns(head):
    return pl.ds(pl.multiple_of(head * HEAD, HEAD), HEAD)


def gather_kernel(
    slots, q_ref, g_ref, k_ref, v_ref, poolk_ref, poolv_ref,
    kv_ref, qg_ref, mem_ref,
    staged, from_core, staged_z, from_z, picked,
    own_sem, a2a_send, a2a_recv, core_sems, z_send, z_recv, m_send, m_recv, hop_send, hop_recv, ring_send, ring_recv,
):
    zl, core, x, y, zh = place()
    head = x * NZ + zh
    up, down = (y + 1) % NY, (y + NY - 1) % NY
    above, below = device(zl, core, x, up, zh), device(zl, core, x, down, zh)
    peers = [device(zl, core, (x + a) % NX, y, (zh + b) % NZ) for a, b in GROUP]
    twin = device(zl, 1 - core, x, y, zh)
    line = [device((zl + a) % ZL, core, x, y, zh) for a in range(ZL)]
    greet(peers[1:] + [above, below, twin] + line[1:])

    def shuffle(base, sources, into):
        out = []
        for i, (a, b) in enumerate(GROUP):
            part = columns(((x + a) % NX) * NZ + (zh + b) % NZ)
            for n, source in enumerate(sources):
                src, dst = source.at[0, :, part], into.at[0, x, n, zh]
                if i == 0:
                    copy = pltpu.make_async_copy(src, dst, own_sem.at[base + n])
                else:
                    at = (base + n, i)
                    copy = remote(src, dst, a2a_send.at[at], a2a_recv.at[at], peers[i])
                copy.start()
                out.append(copy)
        return out

    kv_moves = shuffle(0, (k_ref, v_ref), kv_ref)

    for z in range(ZL):
        for m in range(4):
            row = slots[(z * 2 + (1 - core)) * 4 + m] % 8
            staged[z, 0, m] = poolk_ref[row]
            staged[z, 1, m] = poolv_ref[row]
    to_twin = remote(staged, from_core, core_sems.at[0], core_sems.at[1], twin)
    to_twin.start()

    qg_moves = shuffle(2, (q_ref, g_ref), qg_ref)

    to_twin.wait()
    for z in range(ZL):
        for m in range(4):
            slot = slots[(z * 2 + core) * 4 + m]
            mine = (slot // 8) % 2 == core
            staged_z[z, 0, m] = jnp.where(mine, poolk_ref[slot % 8], from_core[z, 0, m])
            staged_z[z, 1, m] = jnp.where(mine, poolv_ref[slot % 8], from_core[z, 1, m])
    z_moves = []
    for a in range(1, ZL):
        z_moves.append(
            remote(staged_z.at[(zl + a) % ZL], from_z.at[zl], z_send.at[a], z_recv.at[a], line[a])
        )
        z_moves[-1].start()
    from_z[zl] = staged_z[zl]

    def wait_arrival(copy, i):
        if i == 0:
            copy.wait()
        else:
            copy.wait_recv()

    def first_hop(moves, buf, lane, to, shift):
        out = []
        for a in range(NX):
            for i, (pa, pb) in enumerate(GROUP):
                if pa == a:
                    wait_arrival(moves[2 * i], i)
                    wait_arrival(moves[2 * i + 1], i)
            source = (x + NX - a) % NX
            sems = hop_send.at[lane, 0, a], hop_recv.at[lane, 0, a]
            out.append(remote(buf.at[0, source], buf.at[1, (source + shift) % NX], *sems, to))
            out[-1].start()
        return out

    def second_hop(moves, buf, lane, to, arrived, shift):
        out = []
        for a in range(NX):
            moves[a].wait_recv()
            source = (x + NX - a + arrived) % NX
            sems = hop_send.at[lane, 1, a], hop_recv.at[lane, 1, a]
            out.append(remote(buf.at[1, source], buf.at[2, (source + shift) % NX], *sems, to))
            out[-1].start()
        return out

    top, bottom = (y == NY - 1).astype(jnp.int32), (y == 0).astype(jnp.int32)
    kv_hops = first_hop(kv_moves, kv_ref, 0, above, top)
    qg_hops = first_hop(qg_moves, qg_ref, 1, below, (NX - 1) * bottom)
    kv_hops2 = second_hop(kv_hops, kv_ref, 0, above, bottom, top)

    for move in z_moves:
        move.wait_recv()
    for m in range(4):
        owner = slots[((zl * 2 + core) * 4) + m] // 16
        picked[0, m] = from_z[owner, 0, m]
        picked[1, m] = from_z[owner, 1, m]
    m_moves = []
    for i, (a, b) in enumerate(GROUP):
        part = columns(((x + a) % NX) * NZ + (zh + b) % NZ)
        src, dst = picked.at[:, :, :, part], mem_ref.at[y, :, :, head]
        if i == 0:
            copy = pltpu.make_async_copy(src, dst, own_sem.at[4])
        else:
            copy = remote(src, dst, m_send.at[i], m_recv.at[i], peers[i])
        copy.start()
        m_moves.append(copy)

    qg_hops2 = second_hop(qg_hops, qg_ref, 1, below, (NX - 1) * top, (NX - 1) * bottom)

    for i, copy in enumerate(m_moves):
        wait_arrival(copy, i)
    rising, falling = [], []
    for step in range(NY // 2):
        if step:
            rising[-1].wait_recv()
        piece = mem_ref.at[(y + NY - step) % NY]
        rising.append(remote(piece, piece, ring_send.at[0, step], ring_recv.at[0, step], above))
        rising[-1].start()
        if step < NY // 2 - 1:
            if step:
                falling[-1].wait_recv()
            piece = mem_ref.at[(y + step) % NY]
            falling.append(remote(piece, piece, ring_send.at[1, step], ring_recv.at[1, step], below))
            falling[-1].start()
    rising[-1].wait_recv()
    falling[-1].wait_recv()
    for copy in kv_hops2 + qg_hops2:
        copy.wait()
    for copy in kv_moves[2:] + qg_moves[2:] + z_moves + kv_hops + qg_hops + m_moves[1:] + rising + falling:
        copy.wait_send()


def gather(slots, queries, grads, keys, values, poolk, poolv):
    bf16 = jnp.bfloat16
    window = jax.ShapeDtypeStruct((3, NX, 2, NZ, ROWS, HEAD), bf16)
    dma = pltpu.SemaphoreType.DMA
    return pl.pallas_call(
        gather_kernel,
        name="gather",
        out_shape=(window, window, jax.ShapeDtypeStruct((NY, 2, 4, H, 8, HEAD), bf16)),
        in_specs=[SMEM, ANY, ANY, ANY, ANY, VMEM, VMEM],
        out_specs=(ANY, ANY, ANY),
        scratch_shapes=[
            pltpu.VMEM((ZL, 2, 4, 8, H * HEAD), bf16),
            pltpu.VMEM((ZL, 2, 4, 8, H * HEAD), bf16),
            pltpu.VMEM((ZL, 2, 4, 8, H * HEAD), bf16),
            pltpu.VMEM((ZL, 2, 4, 8, H * HEAD), bf16),
            pltpu.VMEM((2, 4, 8, H * HEAD), bf16),
            dma((5,)),
            dma((4, 8)),
            dma((4, 8)),
            dma((2,)),
            dma((ZL,)),
            dma((ZL,)),
            dma((8,)),
            dma((8,)),
            dma((2, 2, NX)),
            dma((2, 2, NX)),
            dma((2, 4)),
            dma((2, 4)),
        ],
        compiler_params=pltpu.CompilerParams(
            collective_id=0, has_side_effects=True, vmem_limit_bytes=24 << 20
        ),
    )(slots, queries, grads, keys, values, poolk, poolv)


SCALE = LOG2E / math.sqrt(HEAD)
NT = (((1,), (1,)), ((), ()))


def dot_nt(a, b):
    return lax.dot_general(a, b, NT, preferred_element_type=jnp.float32)


def dot(a, b):
    return jnp.dot(a, b, preferred_element_type=jnp.float32)


def halves(op, tile):
    return op(tile[:, :HEAD], tile[:, HEAD:])


def attend_kernel(info, q_ref, kv0_ref, kv1_ref, kv2_ref, mem_ref, gq_ref, stat_ref, scores):
    chunk = pl.program_id(0)
    y, length, count = info[0], info[1], info[2]
    base = (chunk * NY + y) * PAIR
    q = q_ref[0, 0, 0]
    row = lax.broadcasted_iota(jnp.int32, (PAIR, PAIR), 0)
    col = lax.broadcasted_iota(jnp.int32, (PAIR, PAIR), 1)
    pos = lax.broadcasted_iota(jnp.int32, (PAIR, HEAD), 0) + base
    g = jnp.where(pos < length, q_ref[0, 0, 1], jnp.zeros((), jnp.bfloat16))
    kv = (kv0_ref, kv1_ref, kv2_ref)
    tiles = 3 + NY

    def key_value(t):
        if t < 3:
            return kv[t][0, 0, 0], kv[t][0, 0, 1]
        return mem_ref[t - 3, 0], mem_ref[t - 3, 1]

    top = None
    for t in range(tiles):
        s = dot_nt(q, key_value(t)[0]) * SCALE
        if t == 0:
            s = jnp.where((col < row) & (base + col < length) | (col == row), s, BARRED)
        elif t == 1:
            s = jnp.where((base >= PAIR) & (base - PAIR + col < length), s, BARRED)
        elif t == 2:
            s = jnp.where((base >= 2 * PAIR) & (base - 2 * PAIR + col < length) & (row < col), s, BARRED)
        else:
            s = jnp.where(col // (PAIR // 4) < count, s, BARRED)
        scores[t] = s
        part = halves(jnp.maximum, s)
        top = part if top is None else jnp.maximum(top, part)
    top = jnp.max(top, axis=1, keepdims=True)
    total = None
    for t in range(tiles):
        e = jnp.exp2(scores[t] - top)
        scores[t] = e
        part = halves(jnp.add, e)
        total = part if total is None else total + part
    total = jnp.sum(total, axis=1, keepdims=True)
    inverse = 1.0 / total
    output = jnp.zeros((PAIR, HEAD), jnp.float32)
    for t in range(tiles):
        prob = scores[t] * inverse
        scores[t] = prob
        output += dot(prob.astype(jnp.bfloat16), key_value(t)[1])
    delta = jnp.sum(g.astype(jnp.float32) * output, axis=1, keepdims=True)
    grad = jnp.zeros((PAIR, HEAD), jnp.float32)
    for t in range(tiles):
        key, value = key_value(t)
        ds = scores[t] * (dot_nt(g, value) - delta)
        grad += dot(ds.astype(jnp.bfloat16), key)
    gq_ref[0] = (grad * (1.0 / math.sqrt(HEAD))).astype(jnp.bfloat16)
    lse = top + jnp.log(total) * LOG2E
    lane = lax.broadcasted_iota(jnp.int32, (PAIR, HEAD), 1)
    both = jnp.where(lane == 0, lse, delta)
    stat_ref[0] = both.T[:8]


def attend(info, qg, kv, mem):
    chunk = (1, 1, 2, PAIR, HEAD)
    return pl.pallas_call(
        attend_kernel,
        name="attend",
        grid_spec=pltpu.PrefetchScalarGridSpec(
            num_scalar_prefetch=1,
            grid=(NX,),
            in_specs=[
                pl.BlockSpec(chunk, lambda i, _: (0, i, 0, 0, 0)),
                pl.BlockSpec(chunk, lambda i, _: (0, i, 0, 0, 0)),
                pl.BlockSpec(chunk, lambda i, _: (1, i, 0, 0, 0)),
                pl.BlockSpec(chunk, lambda i, _: (2, i, 0, 0, 0)),
                pl.BlockSpec((NY, 2, PAIR, HEAD), lambda i, _: (0, 0, 0, 0)),
            ],
            out_specs=[
                pl.BlockSpec((1, PAIR, HEAD), lambda i, _: (i, 0, 0)),
                pl.BlockSpec((1, 8, PAIR), lambda i, _: (i, 0, 0)),
            ],
            scratch_shapes=[pltpu.VMEM((3 + NY, PAIR, PAIR), jnp.float32)],
        ),
        out_shape=(
            jax.ShapeDtypeStruct((NX, PAIR, HEAD), jnp.bfloat16),
            jax.ShapeDtypeStruct((NX, 8, PAIR), jnp.float32),
        ),
        compiler_params=pltpu.CompilerParams(vmem_limit_bytes=40 << 20),
    )(info, qg, kv, kv, kv, mem)


def stats_kernel(stat_ref, out_ref, own_sem, send, recv):
    zl, core, x, y, zh = place()
    backward = [device(zl, core, x, (y + NY - d) % NY, zh) for d in (1, 2)]
    forward = [device(zl, core, x, (y + d) % NY, zh) for d in (1, 2)]
    barrier = pltpu.get_barrier_semaphore()
    for partner in backward + forward:
        pl.semaphore_signal(barrier, inc=1, device_id=partner, device_id_type=MESH)
    pl.semaphore_wait(barrier, 4)
    own = pltpu.make_async_copy(stat_ref, out_ref.at[0], own_sem)
    own.start()
    copies = []
    for d in (1, 2):
        shift = (NX - 1) * (y < d).astype(jnp.int32)
        for c in range(NX):
            copies.append(
                remote(
                    stat_ref.at[c],
                    out_ref.at[d, (c + shift) % NX],
                    send.at[d - 1, c],
                    recv.at[d - 1, c],
                    backward[d - 1],
                )
            )
            copies[-1].start()
    own.wait()
    for copy in copies:
        copy.wait()


def share_stats(stats):
    return pl.pallas_call(
        stats_kernel,
        name="stats",
        out_shape=jax.ShapeDtypeStruct((3, *stats.shape), stats.dtype),
        in_specs=[ANY],
        out_specs=ANY,
        scratch_shapes=[
            pltpu.SemaphoreType.DMA(()),
            pltpu.SemaphoreType.DMA((2, NX)),
            pltpu.SemaphoreType.DMA((2, NX)),
        ],
        compiler_params=pltpu.CompilerParams(collective_id=1, has_side_effects=True),
    )(stats)


def owe_kernel(info, kv_ref, qg_ref, stat_ref, gk_ref, gv_ref):
    chunk = pl.program_id(0)
    y, length = info[0], info[1]
    base = (chunk * NY + y) * PAIR
    key, value = kv_ref[0, 0, 0], kv_ref[0, 0, 1]
    row = lax.broadcasted_iota(jnp.int32, (PAIR, PAIR), 0)
    col = lax.broadcasted_iota(jnp.int32, (PAIR, PAIR), 1)
    pos = lax.broadcasted_iota(jnp.int32, (PAIR, HEAD), 0) + base
    gk = jnp.zeros((PAIR, HEAD), jnp.float32)
    gv = jnp.zeros((PAIR, HEAD), jnp.float32)
    live = base + row < length
    for d in range(3):
        q = qg_ref[d, 0, 0]
        g = jnp.where(pos + d * PAIR < length, qg_ref[d, 0, 1], jnp.zeros((), jnp.bfloat16))
        lse, delta = stat_ref[d, 0, 0:1], stat_ref[d, 0, 1:2]
        s = dot_nt(key, q) * SCALE - lse
        if d == 0:
            allowed = (row < col) & live | (row == col)
        elif d == 1:
            allowed = live & (base + PAIR < NX * NY * PAIR)
        else:
            allowed = live & (base + 2 * PAIR < NX * NY * PAIR) & (col < row)
        prob = jnp.where(allowed, jnp.exp2(jnp.where(allowed, s, BARRED)), 0.0)
        gv += dot(prob.astype(jnp.bfloat16), g)
        ds = prob * (dot_nt(value, g) - delta)
        gk += dot(ds.astype(jnp.bfloat16), q)
    gk_ref[0] = (gk * (1.0 / math.sqrt(HEAD))).astype(jnp.bfloat16)
    gv_ref[0] = gv.astype(jnp.bfloat16)


def owe(info, kv, qg, stats):
    out = jax.ShapeDtypeStruct((NX, PAIR, HEAD), jnp.bfloat16)
    return pl.pallas_call(
        owe_kernel,
        name="owe",
        grid_spec=pltpu.PrefetchScalarGridSpec(
            num_scalar_prefetch=1,
            grid=(NX,),
            in_specs=[
                pl.BlockSpec((1, 1, 2, PAIR, HEAD), lambda i, _: (0, i, 0, 0, 0)),
                pl.BlockSpec((3, 1, 2, PAIR, HEAD), lambda i, _: (0, i, 0, 0, 0)),
                pl.BlockSpec((3, 1, 8, PAIR), lambda i, _: (0, i, 0, 0)),
            ],
            out_specs=[pl.BlockSpec((1, PAIR, HEAD), lambda i, _: (i, 0, 0))] * 2,
        ),
        out_shape=(out, out),
        compiler_params=pltpu.CompilerParams(vmem_limit_bytes=24 << 20),
    )(info, kv, qg, stats)


def scatter_kernel(*refs):
    sources, outs = refs[:3], refs[3:6]
    own_sem, send, recv = refs[6:]
    zl, core, x, y, zh = place()
    peers = [device(zl, core, (x + a) % NX, y, (zh + b) % NZ) for a, b in GROUP]
    greet(peers[1:])
    part = columns(x * NZ + zh)
    local, copies = [], []
    for i, (a, b) in enumerate(GROUP):
        for n in range(3):
            src, dst = sources[n].at[(x + a) % NX, (zh + b) % NZ], outs[n].at[0, :, part]
            if i == 0:
                local.append(pltpu.make_async_copy(src, dst, own_sem.at[n]))
                local[-1].start()
            else:
                copies.append(remote(src, dst, send.at[n, i], recv.at[n, i], peers[i]))
                copies[-1].start()
    for copy in local + copies:
        copy.wait()


def scatter(*parts):
    out = jax.ShapeDtypeStruct((1, ROWS, H * HEAD), jnp.bfloat16)
    return pl.pallas_call(
        scatter_kernel,
        name="scatter",
        out_shape=(out,) * 3,
        in_specs=[ANY] * 3,
        out_specs=(ANY,) * 3,
        scratch_shapes=[
            pltpu.SemaphoreType.DMA((3,)),
            pltpu.SemaphoreType.DMA((3, 8)),
            pltpu.SemaphoreType.DMA((3, 8)),
        ],
        compiler_params=pltpu.CompilerParams(collective_id=2, has_side_effects=True),
    )(*parts)


def on_device(queries, keys, values, grad_out, mem_keys, mem_values, seq_lengths, mem_counts, block_lists, block_slots):
    user = lax.axis_index("dp")
    y = (lax.axis_index("seq") // NZ) % NY
    ids = jnp.arange(block_slots.shape[0], dtype=jnp.int32)
    slots = jnp.sum(
        jnp.where(ids[None, :] == block_lists.reshape(-1)[:, None], block_slots[None, :], 0), axis=1
    )
    mine = jnp.arange(seq_lengths.shape[0]) == user
    info = jnp.stack(
        [y, jnp.sum(jnp.where(mine, seq_lengths, 0)), jnp.sum(jnp.where(mine, mem_counts, 0))]
    ).astype(jnp.int32)
    kv, qg, mem = gather(slots, queries, grad_out, keys, values, mem_keys, mem_values)
    kv = kv.reshape(3, NX, 2, PAIR, HEAD)
    qg = qg.reshape(3, NX, 2, PAIR, HEAD)
    mem = mem.reshape(NY, 2, PAIR, HEAD)
    gq, stats = attend(info, qg, kv, mem)
    gk, gv = owe(info, kv, qg, share_stats(stats))
    split = (NX, NZ, ROWS, HEAD)
    return scatter(gq.reshape(split), gk.reshape(split), gv.reshape(split))


def solution(mesh):
    rows = P("dp", "seq", None)
    return jax.shard_map(
        on_device,
        mesh=mesh,
        in_specs=(rows,) * 6 + (P(),) * 4,
        out_specs=(rows,) * 3,
        check_vma=False,
    )
```

```python
import functools
import math

import jax
import jax.numpy as jnp
from jax import lax
from jax.experimental import pallas as pl
from jax.experimental.pallas import tpu as pltpu
from jax.sharding import PartitionSpec as P

MESH = pl.DeviceIdType.MESH
ANY = pl.BlockSpec(memory_space=pl.ANY)
HBM = pl.BlockSpec(memory_space=pltpu.HBM)
SMEM = pl.BlockSpec(memory_space=pltpu.SMEM)
H = 8
WINDOW = 512
BLK = 512
NX, NY, NZ, ZL = 4, 8, 2, 4
ROWS, HEAD = 128, 128
PAIR = NZ * ROWS
GROUP = [(a, b) for a in range(NX) for b in range(NZ)]
LOG2E = math.log2(math.e)
BARRED = -1e30


def place():
    dp, seq = lax.axis_index("dp"), lax.axis_index("seq")
    return dp // 2, dp % 2, seq // (NY * NZ), (seq // NZ) % NY, seq % NZ


def device(zl, core, x, y, zh):
    return (zl * 2 + core, (x * NY + y) * NZ + zh)


def greet(partners):
    barrier = pltpu.get_barrier_semaphore()
    for partner in partners:
        pl.semaphore_signal(barrier, inc=1, device_id=partner, device_id_type=MESH)
    pl.semaphore_wait(barrier, len(partners))


def remote(src, dst, send, recv, to):
    return pltpu.make_async_remote_copy(
        src_ref=src, dst_ref=dst, send_sem=send, recv_sem=recv, device_id=to, device_id_type=MESH
    )


def columns(head):
    return pl.ds(pl.multiple_of(head * HEAD, HEAD), HEAD)

SCALE = LOG2E / math.sqrt(HEAD)
NT = (((1,), (1,)), ((), ()))


def dot_nt(a, b):
    return lax.dot_general(a, b, NT, preferred_element_type=jnp.float32)


def dot(a, b):
    return jnp.dot(a, b, preferred_element_type=jnp.float32)


def halves(op, tile):
    return op(tile[:, :HEAD], tile[:, HEAD:])


def grid_of(rows, cols):
    return tuple(lax.broadcasted_iota(jnp.int32, (rows, cols), i) for i in range(2))


def attend(base, length, count, q, g, kv_ref, chunk, mem_ref, scores):
    row, col = grid_of(PAIR, PAIR)
    tiles = 3 + NY

    def key_value(t):
        if t < 3:
            return kv_ref[t, chunk, 0], kv_ref[t, chunk, 1]
        return mem_ref[t - 3, 0], mem_ref[t - 3, 1]

    top = None
    for t in range(tiles):
        s = dot_nt(q, key_value(t)[0]) * SCALE
        if t == 0:
            s = jnp.where((col < row) & (base + col < length) | (col == row), s, BARRED)
        elif t == 1:
            s = jnp.where((base >= PAIR) & (base - PAIR + col < length), s, BARRED)
        elif t == 2:
            s = jnp.where((base >= 2 * PAIR) & (base - 2 * PAIR + col < length) & (row < col), s, BARRED)
        else:
            s = jnp.where(col // (PAIR // 4) < count, s, BARRED)
        scores[t] = s
        part = halves(jnp.maximum, s)
        top = part if top is None else jnp.maximum(top, part)
    top = jnp.max(top, axis=1, keepdims=True)
    total = None
    for t in range(tiles):
        e = jnp.exp2(scores[t] - top)
        scores[t] = e
        part = halves(jnp.add, e)
        total = part if total is None else total + part
    total = jnp.sum(total, axis=1, keepdims=True)
    inverse = 1.0 / total
    output = jnp.zeros((PAIR, HEAD), jnp.float32)
    for t in range(tiles):
        prob = scores[t] * inverse
        scores[t] = prob
        output += dot(prob.astype(jnp.bfloat16), key_value(t)[1])
    delta = jnp.sum(g.astype(jnp.float32) * output, axis=1, keepdims=True)
    grad = jnp.zeros((PAIR, HEAD), jnp.float32)
    for t in range(tiles):
        key, value = key_value(t)
        ds = scores[t] * (dot_nt(g, value) - delta)
        grad += dot(ds.astype(jnp.bfloat16), key)
    lse = top + jnp.log(total) * LOG2E
    lane = lax.broadcasted_iota(jnp.int32, (PAIR, HEAD), 1)
    both = jnp.where(lane == 0, lse, delta)
    return (grad * (1.0 / math.sqrt(HEAD))).astype(jnp.bfloat16), both.T[:8]


def owed(d, base, length, key, value, q, g, lse, delta):
    row, col = grid_of(PAIR, PAIR)
    live = base + row < length
    if d == 0:
        allowed = (row < col) & live | (row == col)
    elif d == 1:
        allowed = live & (base + PAIR < NX * NY * PAIR)
    else:
        allowed = live & (base + 2 * PAIR < NX * NY * PAIR) & (col < row)
    s = dot_nt(key, q) * SCALE - lse
    prob = jnp.where(allowed, jnp.exp2(jnp.where(allowed, s, BARRED)), 0.0)
    ds = prob * (dot_nt(value, g) - delta)
    return dot(ds.astype(jnp.bfloat16), q), dot(prob.astype(jnp.bfloat16), g)


def kernel(
    lengths, counts, lists, slots, q_ref, g_ref, k_ref, v_ref, poolk_ref, poolv_ref,
    gq_out, gk_out, gv_out,
    pool, staged, from_core, staged_z, from_z, picked, kv_ref, qg_ref, pieces, mem_ref, scores, stats, grads, sums,
    own_sem, a2a_send, a2a_recv, core_sems, z_send, z_recv, m_send, m_recv, hop_send, hop_recv, ring_send, ring_recv,
    stat_send, stat_recv, out_send, out_recv,
):
    zl, core, x, y, zh = place()
    user = zl * 2 + core
    head = x * NZ + zh
    above, below = [[device(zl, core, x, (y + s * d + NY) % NY, zh) for d in range(3)] for s in (1, -1)]
    peers = [device(zl, core, (x + a) % NX, y, (zh + b) % NZ) for a, b in GROUP]
    twin = device(zl, 1 - core, x, y, zh)
    line = [device((zl + a) % ZL, core, x, y, zh) for a in range(ZL)]
    loads = [
        pltpu.make_async_copy(poolk_ref, pool.at[0], own_sem.at[5]),
        pltpu.make_async_copy(poolv_ref, pool.at[1], own_sem.at[6]),
    ]
    for copy in loads:
        copy.start()
    greet(peers[1:] + above[1:] + below[1:] + [twin] + line[1:])
    ended = []

    def launch(copy):
        copy.start()
        ended.append(copy)
        return copy

    def shuffle(base, sources, into):
        out = []
        for i, (a, b) in enumerate(GROUP):
            part = columns(((x + a) % NX) * NZ + (zh + b) % NZ)
            for n, source in enumerate(sources):
                src, dst = source.at[0, :, part], into.at[0, x, n, pl.ds(pl.multiple_of(zh * ROWS, ROWS), ROWS)]
                if i == 0:
                    out.append(pltpu.make_async_copy(src, dst, own_sem.at[base + n]))
                    out[-1].start()
                else:
                    at = (base + n, i)
                    out.append(launch(remote(src, dst, a2a_send.at[at], a2a_recv.at[at], peers[i])))
        return out

    def arrived(copy, i):
        if i == 0:
            copy.wait()
        else:
            copy.wait_recv()

    def first_hop(moves, buf, lane, to, shift):
        out = []
        for a in range(NX):
            for i, (pa, pb) in enumerate(GROUP):
                if pa == a:
                    arrived(moves[2 * i], i)
                    arrived(moves[2 * i + 1], i)
            source = (x + NX - a) % NX
            sems = hop_send.at[lane, 0, a], hop_recv.at[lane, 0, a]
            out.append(launch(remote(buf.at[0, source], buf.at[1, (source + shift) % NX], *sems, to)))
        return out

    def second_hop(moves, buf, lane, to, before, shift):
        out = []
        for a in range(NX):
            moves[a].wait_recv()
            source = (x + NX - a + before) % NX
            sems = hop_send.at[lane, 1, a], hop_recv.at[lane, 1, a]
            out.append(launch(remote(buf.at[1, source], buf.at[2, (source + shift) % NX], *sems, to)))
        return out

    top, bottom = (y == NY - 1).astype(jnp.int32), (y == 0).astype(jnp.int32)

    kv_moves = shuffle(0, (k_ref, v_ref), kv_ref)

    for copy in loads:
        copy.wait()

    def slot_of(who, m):
        return slots[lists[m, who]]

    for z in range(ZL):
        for m in range(4):
            row = slot_of(z * 2 + (1 - core), m) % 8
            staged[z, 0, m] = pool[0, row]
            staged[z, 1, m] = pool[1, row]
    to_twin = remote(staged, from_core, core_sems.at[0], core_sems.at[1], twin)
    to_twin.start()
    to_twin.wait()
    for z in range(ZL):
        for m in range(4):
            slot = slot_of(z * 2 + core, m)
            mine = (slot // 8) % 2 == core
            staged_z[z, 0, m] = jnp.where(mine, pool[0, slot % 8], from_core[z, 0, m])
            staged_z[z, 1, m] = jnp.where(mine, pool[1, slot % 8], from_core[z, 1, m])
    z_moves = [
        launch(remote(staged_z.at[(zl + a) % ZL], from_z.at[zl], z_send.at[a], z_recv.at[a], line[a]))
        for a in range(1, ZL)
    ]
    from_z[zl] = staged_z[zl]

    kv_hops = first_hop(kv_moves, kv_ref, 0, above[1], top)

    for move in z_moves:
        move.wait_recv()
    for m in range(4):
        owner = slot_of(user, m) // 16
        picked[0, m] = from_z[owner, 0, m]
        picked[1, m] = from_z[owner, 1, m]
    m_moves = []
    for i, (a, b) in enumerate(GROUP):
        part = columns(((x + a) % NX) * NZ + (zh + b) % NZ)
        src, dst = picked.at[:, :, :, part], pieces.at[y, :, :, head]
        if i == 0:
            m_moves.append(pltpu.make_async_copy(src, dst, own_sem.at[4]))
            m_moves[-1].start()
        else:
            m_moves.append(launch(remote(src, dst, m_send.at[i], m_recv.at[i], peers[i])))

    qg_moves = shuffle(2, (q_ref, g_ref), qg_ref)
    kv_hops2 = second_hop(kv_hops, kv_ref, 0, above[1], bottom, top)

    for i, copy in enumerate(m_moves):
        arrived(copy, i)
    rising, falling = [], []
    for step in range(NY // 2):
        if step:
            rising[-1].wait_recv()
        piece = pieces.at[(y + NY - step) % NY]
        rising.append(launch(remote(piece, piece, ring_send.at[0, step], ring_recv.at[0, step], above[1])))
        if step < NY // 2 - 1:
            if step:
                falling[-1].wait_recv()
            piece = pieces.at[(y + step) % NY]
            falling.append(launch(remote(piece, piece, ring_send.at[1, step], ring_recv.at[1, step], below[1])))
        if step == 0:
            qg_hops = first_hop(qg_moves, qg_ref, 1, below[1], (NX - 1) * bottom)
    rising[-1].wait_recv()
    falling[-1].wait_recv()
    for piece in range(NY):
        for n in range(2):
            mem_ref[piece, n] = pieces[piece, n].reshape(PAIR, HEAD)
    for copy in kv_hops2:
        copy.wait_recv()

    length, count = lengths[user], counts[user]
    pos = lax.broadcasted_iota(jnp.int32, (PAIR, HEAD), 0)

    def cotangent(d, chunk, base):
        return jnp.where(pos + base + d * PAIR < length, qg_ref[d, chunk, 1], jnp.zeros((), jnp.bfloat16))

    def base_of(chunk):
        return (chunk * NY + y) * PAIR

    def chunk_at(a):
        return (x + NX - a) % NX

    outs = (gq_out, gk_out, gv_out)
    part = columns(head)

    def piece_out(n, a, b):
        half = (zh + b) % NZ
        chunk = chunk_at(a)
        return remote(
            grads.at[n, chunk, pl.ds(pl.multiple_of(half * ROWS, ROWS), ROWS)],
            outs[n].at[0, :, part],
            out_send.at[n, a, b],
            out_recv.at[n, a, b],
            device(zl, core, chunk, y, half),
        )

    def own_out(n):
        src = grads.at[n, x, pl.ds(pl.multiple_of(zh * ROWS, ROWS), ROWS)]
        return pltpu.make_async_copy(src, outs[n].at[0, :, part], own_sem.at[7 + n])

    def send_out(n, a):
        piece_out(n, a, 1).start()

        @pl.when(a == 0)
        def _():
            own_out(n).start()

        @pl.when(a != 0)
        def _():
            piece_out(n, a, 0).start()

    def stat_out(d, a):
        chunk = chunk_at(a)
        shift = (NX - 1) * (y < d).astype(jnp.int32)
        return remote(
            stats.at[0, chunk],
            stats.at[d, (chunk + shift) % NX],
            stat_send.at[d - 1, a],
            stat_recv.at[d - 1, a],
            below[d],
        )

    def attend_chunk(a, _):
        chunk = chunk_at(a)
        base = base_of(chunk)
        grad, both = attend(
            base, length, count, qg_ref[0, chunk, 0], cotangent(0, chunk, base), kv_ref, chunk, mem_ref, scores
        )
        grads[0, chunk] = grad
        stats[0, chunk] = both
        for d in (1, 2):
            stat_out(d, a).start()
        send_out(0, a)
        return 0

    def contribution(d, chunk):
        base = base_of(chunk)
        return owed(
            d, base, length, kv_ref[0, chunk, 0], kv_ref[0, chunk, 1], qg_ref[d, chunk, 0],
            cotangent(d, chunk, base), stats[d, chunk, 0:1], stats[d, chunk, 1:2],
        )

    def own_chunk(a, _):
        chunk = chunk_at(a)
        sums[0, chunk], sums[1, chunk] = contribution(0, chunk)
        return 0

    def ahead_chunk(a, _):
        chunk = chunk_at(a)
        gk, gv = sums[0, chunk], sums[1, chunk]
        for d in (1, 2):
            more_k, more_v = contribution(d, chunk)
            gk, gv = gk + more_k, gv + more_v
        grads[1, chunk] = (gk * (1.0 / math.sqrt(HEAD))).astype(jnp.bfloat16)
        grads[2, chunk] = gv.astype(jnp.bfloat16)
        send_out(1, a)
        send_out(2, a)
        return 0

    qg_hops2 = second_hop(qg_hops, qg_ref, 1, below[1], (NX - 1) * top, (NX - 1) * bottom)
    lax.fori_loop(0, NX, attend_chunk, 0)
    lax.fori_loop(0, NX, own_chunk, 0)
    for copy in qg_hops2:
        copy.wait_recv()
    for d in (1, 2):
        for a in range(NX):
            stat_out(d, a).wait_recv()
    lax.fori_loop(0, NX, ahead_chunk, 0)

    for n in range(3):
        own_out(n).wait()
        for i, (a, b) in enumerate(GROUP):
            if i:
                piece_out(n, a, b).wait()
    for d in (1, 2):
        for a in range(NX):
            stat_out(d, a).wait_send()
    for copy in ended:
        copy.wait_send()


def backward(lengths, counts, lists, slots, queries, grads, keys, values, poolk, poolv):
    bf16, f32 = jnp.bfloat16, jnp.float32
    out = jax.ShapeDtypeStruct(queries.shape, bf16)
    dma = pltpu.SemaphoreType.DMA
    rows = (8, H * HEAD)
    return pl.pallas_call(
        kernel,
        name="backward",
        out_shape=(out,) * 3,
        in_specs=[SMEM] * 4 + [HBM] * 6,
        out_specs=(ANY,) * 3,
        scratch_shapes=[
            pltpu.VMEM((2, 8, *rows), bf16),
            pltpu.VMEM((ZL, 2, 4, *rows), bf16),
            pltpu.VMEM((ZL, 2, 4, *rows), bf16),
            pltpu.VMEM((ZL, 2, 4, *rows), bf16),
            pltpu.VMEM((ZL, 2, 4, *rows), bf16),
            pltpu.VMEM((2, 4, *rows), bf16),
            pltpu.VMEM((3, NX, 2, PAIR, HEAD), bf16),
            pltpu.VMEM((3, NX, 2, PAIR, HEAD), bf16),
            pltpu.VMEM((NY, 2, 4, H, 8, HEAD), bf16),
            pltpu.VMEM((NY, 2, PAIR, HEAD), bf16),
            pltpu.VMEM((3 + NY, PAIR, PAIR), f32),
            pltpu.VMEM((3, NX, 8, PAIR), f32),
            pltpu.VMEM((3, NX, PAIR, HEAD), bf16),
            pltpu.VMEM((2, NX, PAIR, HEAD), f32),
            dma((10,)),
            dma((4, 8)),
            dma((4, 8)),
            dma((2,)),
            dma((ZL,)),
            dma((ZL,)),
            dma((8,)),
            dma((8,)),
            dma((2, 2, NX)),
            dma((2, 2, NX)),
            dma((2, 4)),
            dma((2, 4)),
            dma((2, NX)),
            dma((2, NX)),
            dma((3, NX, NZ)),
            dma((3, NX, NZ)),
        ],
        compiler_params=pltpu.CompilerParams(
            collective_id=0, has_side_effects=True, vmem_limit_bytes=40 << 20
        ),
    )(lengths, counts, lists, slots, queries, grads, keys, values, poolk, poolv)


def on_device(queries, keys, values, grad_out, mem_keys, mem_values, seq_lengths, mem_counts, block_lists, block_slots):
    return backward(
        seq_lengths, mem_counts, block_lists.T, block_slots, queries, grad_out, keys, values, mem_keys, mem_values
    )


def solution(mesh):
    rows = P("dp", "seq", None)
    return jax.shard_map(
        on_device,
        mesh=mesh,
        in_specs=(rows,) * 6 + (P(),) * 4,
        out_specs=(rows,) * 3,
        check_vma=False,
    )
```

```python
import functools
import math

import jax
import jax.numpy as jnp
from jax import lax
from jax.experimental import pallas as pl
from jax.experimental.pallas import tpu as pltpu
from jax.sharding import PartitionSpec as P

MESH = pl.DeviceIdType.MESH
ANY = pl.BlockSpec(memory_space=pl.ANY)
HBM = pl.BlockSpec(memory_space=pltpu.HBM)
SMEM = pl.BlockSpec(memory_space=pltpu.SMEM)
H = 8
WINDOW = 512
BLK = 512
NX, NY, NZ, ZL = 4, 8, 2, 4
ROWS, HEAD = 128, 128
PAIR = NZ * ROWS
GROUP = [(a, b) for a in range(NX) for b in range(NZ)]
LOG2E = math.log2(math.e)
BARRED = -1e30
UP = 4


def place():
    dp, seq = lax.axis_index("dp"), lax.axis_index("seq")
    return dp // 2, dp % 2, seq // (NY * NZ), (seq // NZ) % NY, seq % NZ


def device(zl, core, x, y, zh):
    return (zl * 2 + core, (x * NY + y) * NZ + zh)


def announce(partners):
    for partner in partners:
        pl.semaphore_signal(
            pltpu.get_barrier_semaphore(), inc=1, device_id=partner, device_id_type=MESH
        )


def remote(src, dst, send, recv, to):
    return pltpu.make_async_remote_copy(
        src_ref=src, dst_ref=dst, send_sem=send, recv_sem=recv, device_id=to, device_id_type=MESH
    )


def columns(head):
    return pl.ds(pl.multiple_of(head * HEAD, HEAD), HEAD)

TILES = 3 + 4 * BLK // PAIR
SCALE = LOG2E / math.sqrt(HEAD)
NT = (((1,), (1,)), ((), ()))


def dot_nt(a, b):
    return lax.dot_general(a, b, NT, preferred_element_type=jnp.float32)


def dot(a, b):
    return jnp.dot(a, b, preferred_element_type=jnp.float32)


def halves(op, tile):
    return op(tile[:, :HEAD], tile[:, HEAD:])


def grid_of(rows, cols):
    return tuple(lax.broadcasted_iota(jnp.int32, (rows, cols), i) for i in range(2))


def weigh(base, length, count, q, key_of, weights):
    row, col = grid_of(PAIR, PAIR)
    top = None
    for t in range(TILES):
        s = dot_nt(q, key_of(t)) * SCALE
        if t == 0:
            s = jnp.where((col < row) & (base + col < length) | (col == row), s, BARRED)
        elif t == 1:
            s = jnp.where((base >= PAIR) & (base - PAIR + col < length), s, BARRED)
        elif t == 2:
            s = jnp.where((base >= 2 * PAIR) & (base - 2 * PAIR + col < length) & (row < col), s, BARRED)
        weights[t] = s
        part = halves(jnp.maximum, s)
        if t >= 3:
            part = jnp.where(block_of(t) < count, part, BARRED)
        top = part if top is None else jnp.maximum(top, part)
    top = jnp.max(top, axis=1, keepdims=True)
    total = None
    for t in range(TILES):
        base_line = top if t < 3 else top + jnp.where(block_of(t) < count, 0.0, -BARRED)
        e = jnp.exp2(weights[t] - base_line)
        weights[t] = e
        part = halves(jnp.add, e)
        total = part if total is None else total + part
    return top, jnp.sum(total, axis=1, keepdims=True)


def block_of(t):
    return (t - 3) // (BLK // PAIR)


def answer(top, total, g, key_of, value_of, weights):
    inverse = 1.0 / total
    output = jnp.zeros((PAIR, HEAD), jnp.float32)
    for t in range(TILES):
        prob = weights[t] * inverse
        output += dot(prob.astype(jnp.bfloat16), value_of(t))
    delta = jnp.sum(g.astype(jnp.float32) * output, axis=1, keepdims=True)
    grad = jnp.zeros((PAIR, HEAD), jnp.float32)
    for t in range(TILES):
        ds = (weights[t] * inverse) * (dot_nt(g, value_of(t)) - delta)
        grad += dot(ds.astype(jnp.bfloat16), key_of(t))
    lse = top + jnp.log(total) * LOG2E
    lane = lax.broadcasted_iota(jnp.int32, (PAIR, HEAD), 1)
    both = jnp.where(lane == 0, lse, delta)
    return (grad * (1.0 / math.sqrt(HEAD))).astype(jnp.bfloat16), both.T[:8]


def owed(d, base, length, key, value, q, g, lse, delta):
    row, col = grid_of(PAIR, PAIR)
    live = base + row < length
    if d == 0:
        allowed = (row < col) & live | (row == col)
    elif d == 1:
        allowed = live & (base + PAIR < NX * NY * PAIR)
    else:
        allowed = live & (base + 2 * PAIR < NX * NY * PAIR) & (col < row)
    s = dot_nt(key, q) * SCALE - lse
    prob = jnp.where(allowed, jnp.exp2(jnp.where(allowed, s, BARRED)), 0.0)
    ds = prob * (dot_nt(value, g) - delta)
    return dot(ds.astype(jnp.bfloat16), q), dot(prob.astype(jnp.bfloat16), g)


def kernel(
    lengths, counts, lists, slots, q_ref, g_ref, k_ref, v_ref, poolk_ref, poolv_ref,
    gq_out, gk_out, gv_out,
    pool0, pool1, staged, from_core, staged_z, from_z0, from_z1, picked, kv_ref, qg_ref, pieces, mem_ref, weights, tops, stats, grads, sums,
    own_sem, a2a_send, a2a_recv, core_sems, z_send, z_recv, m_send, m_recv, hop_send, hop_recv, ring_send, ring_recv,
    stat_send, stat_recv, out_send, out_recv,
):
    zl, core, x, y, zh = place()
    user = zl * 2 + core
    pool, from_z = (pool0, pool1), (from_z0, from_z1)
    head = x * NZ + zh
    above, below = [[device(zl, core, x, (y + s * d + NY) % NY, zh) for d in range(3)] for s in (1, -1)]
    peers = [device(zl, core, (x + a) % NX, y, (zh + b) % NZ) for a, b in GROUP]
    twin = device(zl, 1 - core, x, y, zh)
    line = [device((zl + a) % ZL, core, x, y, zh) for a in range(ZL)]
    loads = [
        pltpu.make_async_copy(poolk_ref, pool0, own_sem.at[5]),
        pltpu.make_async_copy(poolv_ref, pool1, own_sem.at[6]),
    ]
    for copy in loads:
        copy.start()
    partners = peers[1:] + above[1:] + below[1:] + [twin] + line[1:]
    announce(partners)
    ended = []

    def launch(copy):
        copy.start()
        ended.append(copy)
        return copy

    def arrived(copy, i):
        if i == 0:
            copy.wait()
        else:
            copy.wait_recv()

    def chunk_at(a):
        return (x + NX - a) % NX

    class Stream:
        def __init__(self, lane, sources, buf, to, shift, before):
            self.lane, self.sources, self.buf, self.to = lane, sources, buf, to
            self.shift, self.before = shift, before
            self.moves, self.hops = {}, {}

        def shuffle(self, a):
            out = []
            for b in range(NZ):
                i = a * NZ + b
                part = columns(((x + a) % NX) * NZ + (zh + b) % NZ)
                for n, source in enumerate(self.sources):
                    src = source.at[0, :, part]
                    dst = self.buf.at[0, x, n, pl.ds(pl.multiple_of(zh * ROWS, ROWS), ROWS)]
                    k = 2 * self.lane + n
                    if i == 0:
                        out.append((pltpu.make_async_copy(src, dst, own_sem.at[k]), i))
                        out[-1][0].start()
                    else:
                        out.append((launch(remote(src, dst, a2a_send.at[k, i], a2a_recv.at[k, i], peers[i])), i))
            self.moves[a] = out

        def hop(self, step, a):
            if step == 0:
                for copy, i in self.moves[a]:
                    arrived(copy, i)
                source = chunk_at(a)
            else:
                self.hops[0, a].wait_recv()
                source = (chunk_at(a) + self.before) % NX
            sems = hop_send.at[self.lane, step, a], hop_recv.at[self.lane, step, a]
            src, dst = self.buf.at[step, source], self.buf.at[step + 1, (source + self.shift) % NX]
            self.hops[step, a] = launch(remote(src, dst, *sems, self.to))

        def landed(self, a):
            self.hops[1, a].wait_recv()

    top, bottom = (y == NY - 1).astype(jnp.int32), (y == 0).astype(jnp.int32)
    kv = Stream(0, (k_ref, v_ref), kv_ref, above[1], top, bottom)
    qg = Stream(1, (q_ref, g_ref), qg_ref, below[1], (NX - 1) * bottom, (NX - 1) * top)

    def slot_of(who, m):
        return slots[lists[m, who]]

    for n in range(2):
        loads[n].wait()
        for z in range(ZL):
            for m in range(4):
                staged[n, z, m] = pool[n][slot_of(z * 2 + (1 - core), m) % 8]
    pl.semaphore_wait(pltpu.get_barrier_semaphore(), len(partners))

    def to_twin(n):
        return remote(staged.at[n], from_core.at[n], core_sems.at[0, n], core_sems.at[1, n], twin)

    def send_twin():
        for n in range(2):
            launch(to_twin(n))

    def stage_z(n):
        to_twin(n).wait_recv()
        for z in range(ZL):
            for m in range(4):
                slot = slot_of(z * 2 + core, m)
                mine = (slot // 8) % 2 == core
                staged_z[n, z, m] = jnp.where(mine, pool[n][slot % 8], from_core[n, z, m])
        from_z[n][zl] = staged_z[n, zl]

    def z_move(n, a):
        src, dst = staged_z.at[n, (zl + a) % ZL], from_z[n].at[zl]
        return remote(src, dst, z_send.at[n, a], z_recv.at[n, a], line[a])

    def send_z(n):
        for a in range(1, ZL):
            launch(z_move(n, a))

    def m_move(n, i):
        a, b = GROUP[i]
        columns_to = columns(((x + a) % NX) * NZ + (zh + b) % NZ)
        src, dst = picked.at[n, :, :, columns_to], pieces.at[y, n, :, head]
        if i == 0:
            return pltpu.make_async_copy(src, dst, own_sem.at[4 + 6 * n])
        return remote(src, dst, m_send.at[n, i], m_recv.at[n, i], peers[i])

    def send_memory(n):
        for a in range(1, ZL):
            z_move(n, a).wait_recv()
        for m in range(4):
            picked[n, m] = from_z[n][slot_of(user, m) // 16, m]
        m_move(n, 0).start()
        for i in range(1, len(GROUP)):
            launch(m_move(n, i))

    rising, falling = ([], []), ([], [])

    def ring(n, step):
        if step == 0:
            for i in range(len(GROUP)):
                arrived(m_move(n, i), i)
        if step:
            rising[n][-1].wait_recv()
        if step < UP:
            piece = pieces.at[(y + NY - step) % NY, n]
            sems = ring_send.at[n, 0, step], ring_recv.at[n, 0, step]
            rising[n].append(launch(remote(piece, piece, *sems, above[1])))
        if step and step <= NY - 1 - UP:
            falling[n][-1].wait_recv()
        if step < NY - 1 - UP:
            piece = pieces.at[(y + step) % NY, n]
            sems = ring_send.at[n, 1, step], ring_recv.at[n, 1, step]
            falling[n].append(launch(remote(piece, piece, *sems, below[1])))

    kv.shuffle(0)
    kv.shuffle(1)
    kv.shuffle(2)
    kv.shuffle(3)
    send_twin()
    stage_z(0)
    stage_z(1)
    kv.hop(0, 0)
    kv.hop(0, 1)
    qg.shuffle(0)
    qg.shuffle(1)
    kv.hop(0, 2)
    kv.hop(0, 3)
    qg.shuffle(2)
    qg.shuffle(3)
    send_z(0)
    send_z(1)
    kv.hop(1, 0)
    kv.hop(1, 1)
    kv.hop(1, 2)
    qg.hop(0, 0)
    qg.hop(0, 1)
    kv.hop(1, 3)
    qg.hop(0, 2)
    qg.hop(0, 3)
    send_memory(0)
    send_memory(1)
    ring(0, 0)
    ring(1, 0)
    ring(0, 1)
    ring(1, 1)
    qg.hop(1, 0)
    ring(0, 2)
    ring(1, 2)
    qg.hop(1, 1)
    ring(0, 3)
    ring(1, 3)

    def settle(n):
        ring(n, UP)
        for piece in range(NY):
            for m in range(4):
                size = PAIR // 4
                mem_ref[m, n, piece * size : (piece + 1) * size] = pieces[piece, n, m].reshape(size, HEAD)

    settle(0)
    for a in range(NX):
        kv.landed(a)

    length, count = lengths[user], counts[user]
    pos = lax.broadcasted_iota(jnp.int32, (PAIR, HEAD), 0)

    def cotangent(d, chunk, base):
        return jnp.where(pos + base + d * PAIR < length, qg_ref[d, chunk, 1], jnp.zeros((), jnp.bfloat16))

    def base_of(chunk):
        return (chunk * NY + y) * PAIR

    outs = (gq_out, gk_out, gv_out)
    part = columns(head)

    def piece_out(n, a, b):
        half = (zh + b) % NZ
        chunk = chunk_at(a)
        return remote(
            grads.at[n, chunk, pl.ds(pl.multiple_of(half * ROWS, ROWS), ROWS)],
            outs[n].at[0, :, part],
            out_send.at[n, a, b],
            out_recv.at[n, a, b],
            device(zl, core, chunk, y, half),
        )

    def own_out(n):
        src = grads.at[n, x, pl.ds(pl.multiple_of(zh * ROWS, ROWS), ROWS)]
        return pltpu.make_async_copy(src, outs[n].at[0, :, part], own_sem.at[7 + n])

    def send_out(n, a):
        piece_out(n, a, 1).start()

        @pl.when(a == 0)
        def _():
            own_out(n).start()

        @pl.when(a != 0)
        def _():
            piece_out(n, a, 0).start()

    def stat_out(d, a):
        chunk = chunk_at(a)
        shift = (NX - 1) * (y < d).astype(jnp.int32)
        return remote(
            stats.at[0, chunk],
            stats.at[d, (chunk + shift) % NX],
            stat_send.at[d - 1, a],
            stat_recv.at[d - 1, a],
            below[d],
        )

    def tile_of(n, chunk):
        def one(t):
            if t < 3:
                return kv_ref[t, chunk, n]
            half = (t - 3) % (BLK // PAIR)
            return mem_ref[block_of(t), n, half * PAIR : (half + 1) * PAIR]

        return one

    def weigh_chunk(a, _):
        chunk = chunk_at(a)
        top, total = weigh(
            base_of(chunk), length, count, qg_ref[0, chunk, 0], tile_of(0, chunk), weights.at[chunk]
        )
        tops[0, chunk] = jnp.broadcast_to(top, (PAIR, HEAD))
        tops[1, chunk] = jnp.broadcast_to(total, (PAIR, HEAD))
        return 0

    def answer_chunk(a, _):
        chunk = chunk_at(a)
        grad, both = answer(
            tops[0, chunk][:, :1], tops[1, chunk][:, :1], cotangent(0, chunk, base_of(chunk)),
            tile_of(0, chunk), tile_of(1, chunk), weights.at[chunk],
        )
        grads[0, chunk] = grad
        stats[0, chunk] = both
        for d in (1, 2):
            stat_out(d, a).start()
        send_out(0, a)
        return 0

    def contribution(d, chunk):
        base = base_of(chunk)
        return owed(
            d, base, length, kv_ref[0, chunk, 0], kv_ref[0, chunk, 1], qg_ref[d, chunk, 0],
            cotangent(d, chunk, base), stats[d, chunk, 0:1], stats[d, chunk, 1:2],
        )

    def own_chunk(a, _):
        chunk = chunk_at(a)
        sums[0, chunk], sums[1, chunk] = contribution(0, chunk)
        return 0

    def ahead_chunk(a, _):
        chunk = chunk_at(a)
        gk, gv = sums[0, chunk], sums[1, chunk]
        for d in (1, 2):
            more_k, more_v = contribution(d, chunk)
            gk, gv = gk + more_k, gv + more_v
        grads[1, chunk] = (gk * (1.0 / math.sqrt(HEAD))).astype(jnp.bfloat16)
        grads[2, chunk] = gv.astype(jnp.bfloat16)
        send_out(1, a)
        send_out(2, a)
        return 0

    lax.fori_loop(0, 2, weigh_chunk, 0)
    qg.hop(1, 2)
    lax.fori_loop(2, 4, weigh_chunk, 0)
    qg.hop(1, 3)
    settle(1)
    lax.fori_loop(0, 4, answer_chunk, 0)
    lax.fori_loop(0, NX, own_chunk, 0)
    for d in (1, 2):
        for a in range(NX):
            stat_out(d, a).wait_recv()
    turned = (y >= NY - 2).astype(jnp.int32)
    for a in range(NX):
        qg.landed(a)
        ahead_chunk((a + turned) % NX, 0)

    for n in range(3):
        own_out(n).wait()
        for i, (a, b) in enumerate(GROUP):
            if i:
                piece_out(n, a, b).wait()
    for d in (1, 2):
        for a in range(NX):
            stat_out(d, a).wait_send()
    for copy in ended:
        copy.wait_send()


def backward(lengths, counts, lists, slots, queries, grads, keys, values, poolk, poolv):
    bf16, f32 = jnp.bfloat16, jnp.float32
    out = jax.ShapeDtypeStruct(queries.shape, bf16)
    dma = pltpu.SemaphoreType.DMA
    rows = (8, H * HEAD)
    return pl.pallas_call(
        kernel,
        name="backward",
        out_shape=(out,) * 3,
        in_specs=[SMEM] * 4 + [HBM] * 6,
        out_specs=(ANY,) * 3,
        scratch_shapes=[
            pltpu.VMEM((8, *rows), bf16),
            pltpu.VMEM((8, *rows), bf16),
            pltpu.VMEM((2, ZL, 4, *rows), bf16),
            pltpu.VMEM((2, ZL, 4, *rows), bf16),
            pltpu.VMEM((2, ZL, 4, *rows), bf16),
            pltpu.VMEM((ZL, 4, *rows), bf16),
            pltpu.VMEM((ZL, 4, *rows), bf16),
            pltpu.VMEM((2, 4, *rows), bf16),
            pltpu.VMEM((3, NX, 2, PAIR, HEAD), bf16),
            pltpu.VMEM((3, NX, 2, PAIR, HEAD), bf16),
            pltpu.VMEM((NY, 2, 4, H, 8, HEAD), bf16),
            pltpu.VMEM((4, 2, BLK, HEAD), bf16),
            pltpu.VMEM((NX, TILES, PAIR, PAIR), f32),
            pltpu.VMEM((2, NX, PAIR, HEAD), f32),
            pltpu.VMEM((3, NX, 8, PAIR), f32),
            pltpu.VMEM((3, NX, PAIR, HEAD), bf16),
            pltpu.VMEM((2, NX, PAIR, HEAD), f32),
            dma((11,)),
            dma((4, 8)),
            dma((4, 8)),
            dma((2, 2)),
            dma((2, ZL)),
            dma((2, ZL)),
            dma((2, 8)),
            dma((2, 8)),
            dma((2, 2, NX)),
            dma((2, 2, NX)),
            dma((2, 2, UP)),
            dma((2, 2, UP)),
            dma((2, NX)),
            dma((2, NX)),
            dma((3, NX, NZ)),
            dma((3, NX, NZ)),
        ],
        compiler_params=pltpu.CompilerParams(
            collective_id=0, has_side_effects=True, vmem_limit_bytes=60 << 20
        ),
    )(lengths, counts, lists, slots, queries, grads, keys, values, poolk, poolv)


def finish_kernel(*refs):
    for n in range(3):
        refs[3 + n][...] = refs[n][...]


def finish(*parts):
    whole = pl.BlockSpec(memory_space=pltpu.VMEM)
    return pl.pallas_call(
        finish_kernel,
        name="finish",
        out_shape=tuple(jax.ShapeDtypeStruct(part.shape, part.dtype) for part in parts),
        in_specs=[whole] * 3,
        out_specs=(whole,) * 3,
    )(*parts)


def on_device(queries, keys, values, grad_out, mem_keys, mem_values, seq_lengths, mem_counts, block_lists, block_slots):
    parts = backward(
        seq_lengths, mem_counts, block_lists.T, block_slots, queries, grad_out, keys, values, mem_keys, mem_values
    )
    return finish(*parts)


def solution(mesh):
    rows = P("dp", "seq", None)
    return jax.shard_map(
        on_device,
        mesh=mesh,
        in_specs=(rows,) * 6 + (P(),) * 4,
        out_specs=(rows,) * 3,
        check_vma=False,
    )
```

```python
import functools
import math

import jax
import jax.numpy as jnp
from jax import lax
from jax.experimental import pallas as pl
from jax.experimental.pallas import tpu as pltpu
from jax.sharding import PartitionSpec as P

MESH = pl.DeviceIdType.MESH
ANY = pl.BlockSpec(memory_space=pl.ANY)
HBM = pl.BlockSpec(memory_space=pltpu.HBM)
SMEM = pl.BlockSpec(memory_space=pltpu.SMEM)
H = 8
WINDOW = 512
BLK = 512
NX, NY, NZ, ZL = 4, 8, 2, 4
ROWS, HEAD = 128, 128
PAIR = NZ * ROWS
GROUP = [(a, b) for a in range(NX) for b in range(NZ)]
LOG2E = math.log2(math.e)
BARRED = -1e30
UP = 4


def place():
    dp, seq = lax.axis_index("dp"), lax.axis_index("seq")
    return dp // 2, dp % 2, seq // (NY * NZ), (seq // NZ) % NY, seq % NZ


def device(zl, core, x, y, zh):
    return (zl * 2 + core, (x * NY + y) * NZ + zh)


def announce(partners):
    for partner in partners:
        pl.semaphore_signal(
            pltpu.get_barrier_semaphore(), inc=1, device_id=partner, device_id_type=MESH
        )


def remote(src, dst, send, recv, to):
    return pltpu.make_async_remote_copy(
        src_ref=src, dst_ref=dst, send_sem=send, recv_sem=recv, device_id=to, device_id_type=MESH
    )


def columns(head):
    return pl.ds(pl.multiple_of(head * HEAD, HEAD), HEAD)

TILES = 3 + 4 * BLK // PAIR
SCALE = LOG2E / math.sqrt(HEAD)
NT = (((1,), (1,)), ((), ()))


def dot_nt(a, b):
    return lax.dot_general(a, b, NT, preferred_element_type=jnp.float32)


def dot(a, b):
    return jnp.dot(a, b, preferred_element_type=jnp.float32)


def halves(op, tile):
    return op(tile[:, :HEAD], tile[:, HEAD:])


def grid_of(rows, cols):
    return tuple(lax.broadcasted_iota(jnp.int32, (rows, cols), i) for i in range(2))


def weigh(base, length, count, q, key_of, weights):
    row, col = grid_of(PAIR, PAIR)
    top = None
    for t in range(TILES):
        s = dot_nt(q, key_of(t)) * SCALE
        if t == 0:
            s = jnp.where((col < row) & (base + col < length) | (col == row), s, BARRED)
        elif t == 1:
            s = jnp.where((base >= PAIR) & (base - PAIR + col < length), s, BARRED)
        elif t == 2:
            s = jnp.where((base >= 2 * PAIR) & (base - 2 * PAIR + col < length) & (row < col), s, BARRED)
        weights[t] = s
        part = halves(jnp.maximum, s)
        if t >= 3:
            part = jnp.where(block_of(t) < count, part, BARRED)
        top = part if top is None else jnp.maximum(top, part)
    top = jnp.max(top, axis=1, keepdims=True)
    total = None
    for t in range(TILES):
        base_line = top if t < 3 else top + jnp.where(block_of(t) < count, 0.0, -BARRED)
        e = jnp.exp2(weights[t] - base_line)
        weights[t] = e
        part = halves(jnp.add, e)
        total = part if total is None else total + part
    total = jnp.sum(total, axis=1, keepdims=True)
    return top, total, along_lanes(top + jnp.log(total) * LOG2E)


def along_lanes(column):
    return jnp.broadcast_to(column, (PAIR, HEAD)).T[:8]


def block_of(t):
    return (t - 3) // (BLK // PAIR)


def answer(total, g, key_of, value_of, weights):
    inverse = 1.0 / total
    output = jnp.zeros((PAIR, HEAD), jnp.float32)
    for t in range(TILES):
        prob = weights[t] * inverse
        output += dot(prob.astype(jnp.bfloat16), value_of(t))
    delta = jnp.sum(g.astype(jnp.float32) * output, axis=1, keepdims=True)
    grad = jnp.zeros((PAIR, HEAD), jnp.float32)
    for t in range(TILES):
        ds = (weights[t] * inverse) * (dot_nt(g, value_of(t)) - delta)
        grad += dot(ds.astype(jnp.bfloat16), key_of(t))
    return (grad * (1.0 / math.sqrt(HEAD))).astype(jnp.bfloat16), along_lanes(delta)


def seen_again(d, base, length, key, q, lse):
    row, col = grid_of(PAIR, PAIR)
    live = base + row < length
    if d == 0:
        allowed = (row < col) & live | (row == col)
    elif d == 1:
        allowed = live & (base + PAIR < NX * NY * PAIR)
    else:
        allowed = live & (base + 2 * PAIR < NX * NY * PAIR) & (col < row)
    s = dot_nt(key, q) * SCALE - lse
    return jnp.where(allowed, jnp.exp2(jnp.where(allowed, s, BARRED)), 0.0)


def kernel(
    lengths, counts, lists, slots, q_ref, g_ref, k_ref, v_ref, poolk_ref, poolv_ref,
    gq_out, gk_out, gv_out,
    pool0, pool1, staged, from_core, staged_z, from_z0, from_z1, picked, kv_ref, qg_ref, pieces, mem_ref, weights, totals, stats, grads, probs,
    own_sem, a2a_send, a2a_recv, core_sems, z_send, z_recv, m_send, m_recv, hop_send, hop_recv, ring_send, ring_recv,
    stat_send, stat_recv, out_send, out_recv,
):
    zl, core, x, y, zh = place()
    user = zl * 2 + core
    pool, from_z = (pool0, pool1), (from_z0, from_z1)
    head = x * NZ + zh
    above, below = [[device(zl, core, x, (y + s * d + NY) % NY, zh) for d in range(3)] for s in (1, -1)]
    peers = [device(zl, core, (x + a) % NX, y, (zh + b) % NZ) for a, b in GROUP]
    twin = device(zl, 1 - core, x, y, zh)
    line = [device((zl + a) % ZL, core, x, y, zh) for a in range(ZL)]
    loads = [
        pltpu.make_async_copy(poolk_ref, pool0, own_sem.at[5]),
        pltpu.make_async_copy(poolv_ref, pool1, own_sem.at[6]),
    ]
    for copy in loads:
        copy.start()
    partners = peers[1:] + above[1:] + below[1:] + [twin] + line[1:]
    announce(partners)
    ended = []

    def launch(copy):
        copy.start()
        ended.append(copy)
        return copy

    def arrived(copy, i):
        if i == 0:
            copy.wait()
        else:
            copy.wait_recv()

    def chunk_at(a):
        return (x + NX - a) % NX

    class Stream:
        def __init__(self, lane, sources, buf, to, shift, before):
            self.lane, self.sources, self.buf, self.to = lane, sources, buf, to
            self.shift, self.before = shift, before
            self.moves, self.hops = {}, {}

        def shuffle(self, a):
            out = []
            for b in range(NZ):
                i = a * NZ + b
                part = columns(((x + a) % NX) * NZ + (zh + b) % NZ)
                for n, source in enumerate(self.sources):
                    src = source.at[0, :, part]
                    dst = self.buf.at[0, x, n, pl.ds(pl.multiple_of(zh * ROWS, ROWS), ROWS)]
                    k = 2 * self.lane + n
                    if i == 0:
                        out.append((pltpu.make_async_copy(src, dst, own_sem.at[k]), i))
                        out[-1][0].start()
                    else:
                        out.append((launch(remote(src, dst, a2a_send.at[k, i], a2a_recv.at[k, i], peers[i])), i))
            self.moves[a] = out

        def hop(self, step, a):
            if step == 0:
                for copy, i in self.moves[a]:
                    arrived(copy, i)
                source = chunk_at(a)
            else:
                self.hops[0, a].wait_recv()
                source = (chunk_at(a) + self.before) % NX
            sems = hop_send.at[self.lane, step, a], hop_recv.at[self.lane, step, a]
            src, dst = self.buf.at[step, source], self.buf.at[step + 1, (source + self.shift) % NX]
            self.hops[step, a] = launch(remote(src, dst, *sems, self.to))

        def landed(self, a):
            self.hops[1, a].wait_recv()

    top, bottom = (y == NY - 1).astype(jnp.int32), (y == 0).astype(jnp.int32)
    kv = Stream(0, (k_ref, v_ref), kv_ref, above[1], top, bottom)
    qg = Stream(1, (q_ref, g_ref), qg_ref, below[1], (NX - 1) * bottom, (NX - 1) * top)

    def slot_of(who, m):
        return slots[lists[m, who]]

    for n in range(2):
        loads[n].wait()
        for z in range(ZL):
            for m in range(4):
                staged[n, z, m] = pool[n][slot_of(z * 2 + (1 - core), m) % 8]
    pl.semaphore_wait(pltpu.get_barrier_semaphore(), len(partners))

    def to_twin(n):
        return remote(staged.at[n], from_core.at[n], core_sems.at[0, n], core_sems.at[1, n], twin)

    def send_twin():
        for n in range(2):
            launch(to_twin(n))

    def stage_z(n):
        to_twin(n).wait_recv()
        for z in range(ZL):
            for m in range(4):
                slot = slot_of(z * 2 + core, m)
                mine = (slot // 8) % 2 == core
                staged_z[n, z, m] = jnp.where(mine, pool[n][slot % 8], from_core[n, z, m])
        from_z[n][zl] = staged_z[n, zl]

    def z_move(n, a):
        src, dst = staged_z.at[n, (zl + a) % ZL], from_z[n].at[zl]
        return remote(src, dst, z_send.at[n, a], z_recv.at[n, a], line[a])

    def send_z(n):
        for a in range(1, ZL):
            launch(z_move(n, a))

    def m_move(n, i):
        a, b = GROUP[i]
        columns_to = columns(((x + a) % NX) * NZ + (zh + b) % NZ)
        src, dst = picked.at[n, :, :, columns_to], pieces.at[y, n, :, head]
        if i == 0:
            return pltpu.make_async_copy(src, dst, own_sem.at[4 + 6 * n])
        return remote(src, dst, m_send.at[n, i], m_recv.at[n, i], peers[i])

    def send_memory(n):
        for a in range(1, ZL):
            z_move(n, a).wait_recv()
        for m in range(4):
            picked[n, m] = from_z[n][slot_of(user, m) // 16, m]
        m_move(n, 0).start()
        for i in range(1, len(GROUP)):
            launch(m_move(n, i))

    rising, falling = ([], []), ([], [])

    def ring(n, step):
        if step == 0:
            for i in range(len(GROUP)):
                arrived(m_move(n, i), i)
        if step:
            rising[n][-1].wait_recv()
        if step < UP:
            piece = pieces.at[(y + NY - step) % NY, n]
            sems = ring_send.at[n, 0, step], ring_recv.at[n, 0, step]
            rising[n].append(launch(remote(piece, piece, *sems, above[1])))
        if step and step <= NY - 1 - UP:
            falling[n][-1].wait_recv()
        if step < NY - 1 - UP:
            piece = pieces.at[(y + step) % NY, n]
            sems = ring_send.at[n, 1, step], ring_recv.at[n, 1, step]
            falling[n].append(launch(remote(piece, piece, *sems, below[1])))

    kv.shuffle(0)
    kv.shuffle(1)
    kv.shuffle(2)
    kv.shuffle(3)
    send_twin()
    stage_z(0)
    stage_z(1)
    kv.hop(0, 0)
    kv.hop(0, 1)
    qg.shuffle(0)
    qg.shuffle(1)
    kv.hop(0, 2)
    kv.hop(0, 3)
    qg.shuffle(2)
    qg.shuffle(3)
    send_z(0)
    send_z(1)
    kv.hop(1, 0)
    kv.hop(1, 1)
    kv.hop(1, 2)
    qg.hop(0, 0)
    qg.hop(0, 1)
    kv.hop(1, 3)
    qg.hop(0, 2)
    qg.hop(0, 3)
    send_memory(0)
    send_memory(1)
    ring(0, 0)
    ring(1, 0)
    ring(0, 1)
    ring(1, 1)
    qg.hop(1, 0)
    ring(0, 2)
    ring(1, 2)
    qg.hop(1, 1)
    ring(0, 3)
    ring(1, 3)

    def settle(n):
        ring(n, UP)
        for piece in range(NY):
            for m in range(4):
                size = PAIR // 4
                mem_ref[m, n, piece * size : (piece + 1) * size] = pieces[piece, n, m].reshape(size, HEAD)

    settle(0)
    for a in range(NX):
        kv.landed(a)

    length, count = lengths[user], counts[user]
    pos = lax.broadcasted_iota(jnp.int32, (PAIR, HEAD), 0)

    def cotangent(d, chunk, base):
        return jnp.where(pos + base + d * PAIR < length, qg_ref[d, chunk, 1], jnp.zeros((), jnp.bfloat16))

    def base_of(chunk):
        return (chunk * NY + y) * PAIR

    outs = (gq_out, gk_out, gv_out)
    part = columns(head)

    def piece_out(n, a, b):
        half = (zh + b) % NZ
        chunk = chunk_at(a)
        return remote(
            grads.at[n, chunk, pl.ds(pl.multiple_of(half * ROWS, ROWS), ROWS)],
            outs[n].at[0, :, part],
            out_send.at[n, a, b],
            out_recv.at[n, a, b],
            device(zl, core, chunk, y, half),
        )

    def own_out(n):
        src = grads.at[n, x, pl.ds(pl.multiple_of(zh * ROWS, ROWS), ROWS)]
        return pltpu.make_async_copy(src, outs[n].at[0, :, part], own_sem.at[7 + n])

    def send_out(n, a):
        piece_out(n, a, 1).start()

        @pl.when(a == 0)
        def _():
            own_out(n).start()

        @pl.when(a != 0)
        def _():
            piece_out(n, a, 0).start()

    def stat_out(kind, d, a):
        chunk = chunk_at(a)
        shift = (NX - 1) * (y < d).astype(jnp.int32)
        sems = stat_send.at[kind, d - 1, a], stat_recv.at[kind, d - 1, a]
        return remote(stats.at[kind, 0, chunk], stats.at[kind, d, (chunk + shift) % NX], *sems, below[d])

    def share(kind, chunk, a, stat):
        stats[kind, 0, chunk] = stat
        for d in (1, 2):
            stat_out(kind, d, a).start()

    def shared(kind):
        for d in (1, 2):
            for a in range(NX):
                stat_out(kind, d, a).wait_recv()

    def tile_of(n, chunk):
        def one(t):
            if t < 3:
                return kv_ref[t, chunk, n]
            half = (t - 3) % (BLK // PAIR)
            return mem_ref[block_of(t), n, half * PAIR : (half + 1) * PAIR]

        return one

    def weigh_chunk(a, _):
        chunk = chunk_at(a)
        _, total, lse = weigh(
            base_of(chunk), length, count, qg_ref[0, chunk, 0], tile_of(0, chunk), weights.at[chunk]
        )
        totals[chunk] = jnp.broadcast_to(total, (PAIR, HEAD))
        share(0, chunk, a, lse)
        return 0

    def answer_chunk(a, _):
        chunk = chunk_at(a)
        grad, delta = answer(
            totals[chunk][:, :1], cotangent(0, chunk, base_of(chunk)),
            tile_of(0, chunk), tile_of(1, chunk), weights.at[chunk],
        )
        grads[0, chunk] = grad
        share(1, chunk, a, delta)
        send_out(0, a)
        return 0

    def value_chunk(a):
        chunk = chunk_at(a)
        base = base_of(chunk)
        gv = jnp.zeros((PAIR, HEAD), jnp.float32)
        for d in range(3):
            prob = seen_again(
                d, base, length, kv_ref[0, chunk, 0], qg_ref[d, chunk, 0], stats[0, d, chunk, 0:1]
            )
            probs[chunk, d] = prob
            gv += dot(prob.astype(jnp.bfloat16), cotangent(d, chunk, base))
        grads[2, chunk] = gv.astype(jnp.bfloat16)
        send_out(2, a)

    def key_chunk(a, _):
        chunk = chunk_at(a)
        base = base_of(chunk)
        gk = jnp.zeros((PAIR, HEAD), jnp.float32)
        for d in range(3):
            dprob = dot_nt(kv_ref[0, chunk, 1], cotangent(d, chunk, base))
            ds = probs[chunk, d] * (dprob - stats[1, d, chunk, 0:1])
            gk += dot(ds.astype(jnp.bfloat16), qg_ref[d, chunk, 0])
        grads[1, chunk] = (gk * (1.0 / math.sqrt(HEAD))).astype(jnp.bfloat16)
        send_out(1, a)
        return 0

    lax.fori_loop(0, 2, weigh_chunk, 0)
    qg.hop(1, 2)
    lax.fori_loop(2, 4, weigh_chunk, 0)
    qg.hop(1, 3)
    settle(1)
    lax.fori_loop(0, 4, answer_chunk, 0)
    shared(0)
    turned = (y >= NY - 2).astype(jnp.int32)
    for a in range(NX):
        qg.landed(a)
        value_chunk((a + turned) % NX)
    shared(1)
    lax.fori_loop(0, NX, key_chunk, 0)

    for n in range(3):
        own_out(n).wait()
        for i, (a, b) in enumerate(GROUP):
            if i:
                piece_out(n, a, b).wait()
    for kind in range(2):
        for d in (1, 2):
            for a in range(NX):
                stat_out(kind, d, a).wait_send()
    for copy in ended:
        copy.wait_send()


def backward(lengths, counts, lists, slots, queries, grads, keys, values, poolk, poolv):
    bf16, f32 = jnp.bfloat16, jnp.float32
    out = jax.ShapeDtypeStruct(queries.shape, bf16)
    dma = pltpu.SemaphoreType.DMA
    rows = (8, H * HEAD)
    return pl.pallas_call(
        kernel,
        name="backward",
        out_shape=(out,) * 3,
        in_specs=[SMEM] * 4 + [HBM] * 6,
        out_specs=(ANY,) * 3,
        scratch_shapes=[
            pltpu.VMEM((8, *rows), bf16),
            pltpu.VMEM((8, *rows), bf16),
            pltpu.VMEM((2, ZL, 4, *rows), bf16),
            pltpu.VMEM((2, ZL, 4, *rows), bf16),
            pltpu.VMEM((2, ZL, 4, *rows), bf16),
            pltpu.VMEM((ZL, 4, *rows), bf16),
            pltpu.VMEM((ZL, 4, *rows), bf16),
            pltpu.VMEM((2, 4, *rows), bf16),
            pltpu.VMEM((3, NX, 2, PAIR, HEAD), bf16),
            pltpu.VMEM((3, NX, 2, PAIR, HEAD), bf16),
            pltpu.VMEM((NY, 2, 4, H, 8, HEAD), bf16),
            pltpu.VMEM((4, 2, BLK, HEAD), bf16),
            pltpu.VMEM((NX, TILES, PAIR, PAIR), f32),
            pltpu.VMEM((NX, PAIR, HEAD), f32),
            pltpu.VMEM((2, 3, NX, 8, PAIR), f32),
            pltpu.VMEM((3, NX, PAIR, HEAD), bf16),
            pltpu.VMEM((NX, 3, PAIR, PAIR), f32),
            dma((11,)),
            dma((4, 8)),
            dma((4, 8)),
            dma((2, 2)),
            dma((2, ZL)),
            dma((2, ZL)),
            dma((2, 8)),
            dma((2, 8)),
            dma((2, 2, NX)),
            dma((2, 2, NX)),
            dma((2, 2, UP)),
            dma((2, 2, UP)),
            dma((2, 2, NX)),
            dma((2, 2, NX)),
            dma((3, NX, NZ)),
            dma((3, NX, NZ)),
        ],
        compiler_params=pltpu.CompilerParams(
            collective_id=0, has_side_effects=True, vmem_limit_bytes=60 << 20
        ),
    )(lengths, counts, lists, slots, queries, grads, keys, values, poolk, poolv)


def finish_kernel(*refs):
    for n in range(3):
        refs[3 + n][...] = refs[n][...]


def finish(*parts):
    whole = pl.BlockSpec(memory_space=pltpu.VMEM)
    return pl.pallas_call(
        finish_kernel,
        name="finish",
        out_shape=tuple(jax.ShapeDtypeStruct(part.shape, part.dtype) for part in parts),
        in_specs=[whole] * 3,
        out_specs=(whole,) * 3,
    )(*parts)


def on_device(queries, keys, values, grad_out, mem_keys, mem_values, seq_lengths, mem_counts, block_lists, block_slots):
    parts = backward(
        seq_lengths, mem_counts, block_lists.T, block_slots, queries, grad_out, keys, values, mem_keys, mem_values
    )
    return finish(*parts)


def solution(mesh):
    rows = P("dp", "seq", None)
    return jax.shard_map(
        on_device,
        mesh=mesh,
        in_specs=(rows,) * 6 + (P(),) * 4,
        out_specs=(rows,) * 3,
        check_vma=False,
    )
```

```python
import functools
import math

import jax
import jax.numpy as jnp
from jax import lax
from jax.experimental import pallas as pl
from jax.experimental.pallas import tpu as pltpu
from jax.sharding import PartitionSpec as P

MESH = pl.DeviceIdType.MESH
ANY = pl.BlockSpec(memory_space=pl.ANY)
HBM = pl.BlockSpec(memory_space=pltpu.HBM)
SMEM = pl.BlockSpec(memory_space=pltpu.SMEM)
H = 8
WINDOW = 512
BLK = 512
NX, NY, NZ, ZL = 4, 8, 2, 4
ROWS, HEAD = 128, 128
PAIR = NZ * ROWS
GROUP = [(a, b) for a in range(NX) for b in range(NZ)]
LOG2E = math.log2(math.e)
BARRED = -1e30
UP = 4


def place():
    dp, seq = lax.axis_index("dp"), lax.axis_index("seq")
    return dp // 2, dp % 2, seq // (NY * NZ), (seq // NZ) % NY, seq % NZ


def device(zl, core, x, y, zh):
    return (zl * 2 + core, (x * NY + y) * NZ + zh)


def announce(partners):
    for partner in partners:
        pl.semaphore_signal(
            pltpu.get_barrier_semaphore(), inc=1, device_id=partner, device_id_type=MESH
        )


def remote(src, dst, send, recv, to):
    return pltpu.make_async_remote_copy(
        src_ref=src, dst_ref=dst, send_sem=send, recv_sem=recv, device_id=to, device_id_type=MESH
    )


def columns(head):
    return pl.ds(pl.multiple_of(head * HEAD, HEAD), HEAD)

TILES = 3 + 4 * BLK // PAIR
SCALE = LOG2E / math.sqrt(HEAD)
NT = (((1,), (1,)), ((), ()))


def dot_nt(a, b):
    return lax.dot_general(a, b, NT, preferred_element_type=jnp.float32)


def dot(a, b):
    return jnp.dot(a, b, preferred_element_type=jnp.float32)


def halves(op, tile):
    return op(tile[:, :HEAD], tile[:, HEAD:])


def grid_of(rows, cols):
    return tuple(lax.broadcasted_iota(jnp.int32, (rows, cols), i) for i in range(2))


def weigh(base, length, count, q, key_of, weights):
    row, col = grid_of(PAIR, PAIR)
    top = None
    for t in range(TILES):
        s = dot_nt(q, key_of(t)) * SCALE
        if t == 0:
            s = jnp.where((col < row) & (base + col < length) | (col == row), s, BARRED)
        elif t == 1:
            s = jnp.where((base >= PAIR) & (base - PAIR + col < length), s, BARRED)
        elif t == 2:
            s = jnp.where((base >= 2 * PAIR) & (base - 2 * PAIR + col < length) & (row < col), s, BARRED)
        weights[t] = s
        part = halves(jnp.maximum, s)
        if t >= 3:
            part = jnp.where(block_of(t) < count, part, BARRED)
        top = part if top is None else jnp.maximum(top, part)
    top = jnp.max(top, axis=1, keepdims=True)
    total = None
    for t in range(TILES):
        base_line = top if t < 3 else top + jnp.where(block_of(t) < count, 0.0, -BARRED)
        e = jnp.exp2(weights[t] - base_line)
        weights[t] = e
        part = halves(jnp.add, e)
        total = part if total is None else total + part
    total = jnp.sum(total, axis=1, keepdims=True)
    return top, total, along_lanes(top + jnp.log(total) * LOG2E)


def along_lanes(column):
    return jnp.broadcast_to(column, (PAIR, HEAD)).T[:8]


def block_of(t):
    return (t - 3) // (BLK // PAIR)


def answer(total, g, key_of, value_of, weights, dprobs):
    inverse = 1.0 / total
    delta = None
    for t in range(TILES):
        half = (weights[t] * inverse).astype(jnp.bfloat16)
        dprob = dot_nt(g, value_of(t))
        dprobs[t] = dprob
        part = halves(jnp.add, half.astype(jnp.float32) * dprob)
        delta = part if delta is None else delta + part
    delta = jnp.sum(delta, axis=1, keepdims=True)
    grad = jnp.zeros((PAIR, HEAD), jnp.float32)
    for t in range(TILES):
        ds = (weights[t] * inverse) * (dprobs[t] - delta)
        grad += dot(ds.astype(jnp.bfloat16), key_of(t))
    return (grad * (1.0 / math.sqrt(HEAD))).astype(jnp.bfloat16), along_lanes(delta)


def seen_again(d, base, length, key, q, lse):
    row, col = grid_of(PAIR, PAIR)
    live = base + row < length
    if d == 0:
        allowed = (row < col) & live | (row == col)
    elif d == 1:
        allowed = live & (base + PAIR < NX * NY * PAIR)
    else:
        allowed = live & (base + 2 * PAIR < NX * NY * PAIR) & (col < row)
    s = dot_nt(key, q) * SCALE - lse
    return jnp.where(allowed, jnp.exp2(jnp.where(allowed, s, BARRED)), 0.0)


def kernel(
    lengths, counts, lists, slots, q_ref, g_ref, k_ref, v_ref, poolk_ref, poolv_ref,
    gq_out, gk_out, gv_out,
    pool0, pool1, staged, from_core, staged_z, from_z0, from_z1, picked, kv_ref, qg_ref, pieces, mem_ref, weights, dprobs, totals, stats, grads, probs,
    own_sem, a2a_send, a2a_recv, core_sems, z_send, z_recv, m_send, m_recv, hop_send, hop_recv, ring_send, ring_recv,
    stat_send, stat_recv, out_send, out_recv,
):
    zl, core, x, y, zh = place()
    user = zl * 2 + core
    pool, from_z = (pool0, pool1), (from_z0, from_z1)
    head = x * NZ + zh
    above, below = [[device(zl, core, x, (y + s * d + NY) % NY, zh) for d in range(3)] for s in (1, -1)]
    peers = [device(zl, core, (x + a) % NX, y, (zh + b) % NZ) for a, b in GROUP]
    twin = device(zl, 1 - core, x, y, zh)
    line = [device((zl + a) % ZL, core, x, y, zh) for a in range(ZL)]
    loads = [
        pltpu.make_async_copy(poolk_ref, pool0, own_sem.at[5]),
        pltpu.make_async_copy(poolv_ref, pool1, own_sem.at[6]),
    ]
    for copy in loads:
        copy.start()
    partners = peers[1:] + above[1:] + below[1:] + [twin] + line[1:]
    announce(partners)
    ended = []

    def launch(copy):
        copy.start()
        ended.append(copy)
        return copy

    def arrived(copy, i):
        if i == 0:
            copy.wait()
        else:
            copy.wait_recv()

    def chunk_at(a):
        return (x + NX - a) % NX

    class Stream:
        def __init__(self, lane, sources, buf, to, shift, before):
            self.lane, self.sources, self.buf, self.to = lane, sources, buf, to
            self.shift, self.before = shift, before
            self.moves, self.hops = {}, {}

        def shuffle(self, a):
            out = []
            for b in range(NZ):
                i = a * NZ + b
                part = columns(((x + a) % NX) * NZ + (zh + b) % NZ)
                for n, source in enumerate(self.sources):
                    src = source.at[0, :, part]
                    dst = self.buf.at[0, x, n, pl.ds(pl.multiple_of(zh * ROWS, ROWS), ROWS)]
                    k = 2 * self.lane + n
                    if i == 0:
                        out.append((pltpu.make_async_copy(src, dst, own_sem.at[k]), i))
                        out[-1][0].start()
                    else:
                        out.append((launch(remote(src, dst, a2a_send.at[k, i], a2a_recv.at[k, i], peers[i])), i))
            self.moves[a] = out

        def hop(self, step, a):
            if step == 0:
                for copy, i in self.moves[a]:
                    arrived(copy, i)
                source = chunk_at(a)
            else:
                self.hops[0, a].wait_recv()
                source = (chunk_at(a) + self.before) % NX
            sems = hop_send.at[self.lane, step, a], hop_recv.at[self.lane, step, a]
            src, dst = self.buf.at[step, source], self.buf.at[step + 1, (source + self.shift) % NX]
            self.hops[step, a] = launch(remote(src, dst, *sems, self.to))

        def landed(self, a):
            self.hops[1, a].wait_recv()

    top, bottom = (y == NY - 1).astype(jnp.int32), (y == 0).astype(jnp.int32)
    kv = Stream(0, (k_ref, v_ref), kv_ref, above[1], top, bottom)
    qg = Stream(1, (q_ref, g_ref), qg_ref, below[1], (NX - 1) * bottom, (NX - 1) * top)

    def slot_of(who, m):
        return slots[lists[m, who]]

    for n in range(2):
        loads[n].wait()
        for z in range(ZL):
            for m in range(4):
                staged[n, z, m] = pool[n][slot_of(z * 2 + (1 - core), m) % 8]
    pl.semaphore_wait(pltpu.get_barrier_semaphore(), len(partners))

    def to_twin(n):
        return remote(staged.at[n], from_core.at[n], core_sems.at[0, n], core_sems.at[1, n], twin)

    def send_twin():
        for n in range(2):
            launch(to_twin(n))

    def stage_z(n):
        to_twin(n).wait_recv()
        for z in range(ZL):
            for m in range(4):
                slot = slot_of(z * 2 + core, m)
                mine = (slot // 8) % 2 == core
                staged_z[n, z, m] = jnp.where(mine, pool[n][slot % 8], from_core[n, z, m])
        from_z[n][zl] = staged_z[n, zl]

    def z_move(n, a):
        src, dst = staged_z.at[n, (zl + a) % ZL], from_z[n].at[zl]
        return remote(src, dst, z_send.at[n, a], z_recv.at[n, a], line[a])

    def send_z(n):
        for a in range(1, ZL):
            launch(z_move(n, a))

    def m_move(n, i):
        a, b = GROUP[i]
        columns_to = columns(((x + a) % NX) * NZ + (zh + b) % NZ)
        src, dst = picked.at[n, :, :, columns_to], pieces.at[y, n, :, head]
        if i == 0:
            return pltpu.make_async_copy(src, dst, own_sem.at[4 + 6 * n])
        return remote(src, dst, m_send.at[n, i], m_recv.at[n, i], peers[i])

    def send_memory(n):
        for a in range(1, ZL):
            z_move(n, a).wait_recv()
        for m in range(4):
            picked[n, m] = from_z[n][slot_of(user, m) // 16, m]
        m_move(n, 0).start()
        for i in range(1, len(GROUP)):
            launch(m_move(n, i))

    rising, falling = ([], []), ([], [])

    def ring(n, step):
        if step == 0:
            for i in range(len(GROUP)):
                arrived(m_move(n, i), i)
        if step:
            rising[n][-1].wait_recv()
        if step < UP:
            piece = pieces.at[(y + NY - step) % NY, n]
            sems = ring_send.at[n, 0, step], ring_recv.at[n, 0, step]
            rising[n].append(launch(remote(piece, piece, *sems, above[1])))
        if step and step <= NY - 1 - UP:
            falling[n][-1].wait_recv()
        if step < NY - 1 - UP:
            piece = pieces.at[(y + step) % NY, n]
            sems = ring_send.at[n, 1, step], ring_recv.at[n, 1, step]
            falling[n].append(launch(remote(piece, piece, *sems, below[1])))

    kv.shuffle(0)
    kv.shuffle(1)
    kv.shuffle(2)
    kv.shuffle(3)
    send_twin()
    stage_z(0)
    stage_z(1)
    kv.hop(0, 0)
    kv.hop(0, 1)
    qg.shuffle(0)
    qg.shuffle(1)
    kv.hop(0, 2)
    kv.hop(0, 3)
    qg.shuffle(2)
    qg.shuffle(3)
    send_z(0)
    send_z(1)
    kv.hop(1, 0)
    kv.hop(1, 1)
    kv.hop(1, 2)
    qg.hop(0, 0)
    qg.hop(0, 1)
    kv.hop(1, 3)
    qg.hop(0, 2)
    qg.hop(0, 3)
    send_memory(0)
    send_memory(1)
    ring(0, 0)
    ring(1, 0)
    ring(0, 1)
    ring(1, 1)
    qg.hop(1, 0)
    ring(0, 2)
    ring(1, 2)
    qg.hop(1, 1)
    ring(0, 3)
    ring(1, 3)

    def settle(n):
        ring(n, UP)
        for piece in range(NY):
            for m in range(4):
                size = PAIR // 4
                mem_ref[m, n, piece * size : (piece + 1) * size] = pieces[piece, n, m].reshape(size, HEAD)

    settle(0)
    for a in range(NX):
        kv.landed(a)

    length, count = lengths[user], counts[user]
    pos = lax.broadcasted_iota(jnp.int32, (PAIR, HEAD), 0)

    def cotangent(d, chunk, base):
        return jnp.where(pos + base + d * PAIR < length, qg_ref[d, chunk, 1], jnp.zeros((), jnp.bfloat16))

    def base_of(chunk):
        return (chunk * NY + y) * PAIR

    outs = (gq_out, gk_out, gv_out)
    part = columns(head)

    def piece_out(n, a, b):
        half = (zh + b) % NZ
        chunk = chunk_at(a)
        return remote(
            grads.at[n, chunk, pl.ds(pl.multiple_of(half * ROWS, ROWS), ROWS)],
            outs[n].at[0, :, part],
            out_send.at[n, a, b],
            out_recv.at[n, a, b],
            device(zl, core, chunk, y, half),
        )

    def own_out(n):
        src = grads.at[n, x, pl.ds(pl.multiple_of(zh * ROWS, ROWS), ROWS)]
        return pltpu.make_async_copy(src, outs[n].at[0, :, part], own_sem.at[7 + n])

    def send_out(n, a):
        piece_out(n, a, 1).start()

        @pl.when(a == 0)
        def _():
            own_out(n).start()

        @pl.when(a != 0)
        def _():
            piece_out(n, a, 0).start()

    def stat_out(kind, d, a):
        chunk = chunk_at(a)
        shift = (NX - 1) * (y < d).astype(jnp.int32)
        sems = stat_send.at[kind, d - 1, a], stat_recv.at[kind, d - 1, a]
        return remote(stats.at[kind, 0, chunk], stats.at[kind, d, (chunk + shift) % NX], *sems, below[d])

    def share(kind, chunk, a, stat):
        stats[kind, 0, chunk] = stat
        for d in (1, 2):
            stat_out(kind, d, a).start()

    def shared(kind):
        for d in (1, 2):
            for a in range(NX):
                stat_out(kind, d, a).wait_recv()

    def tile_of(n, chunk):
        def one(t):
            if t < 3:
                return kv_ref[t, chunk, n]
            half = (t - 3) % (BLK // PAIR)
            return mem_ref[block_of(t), n, half * PAIR : (half + 1) * PAIR]

        return one

    def weigh_chunk(a, _):
        chunk = chunk_at(a)
        _, total, lse = weigh(
            base_of(chunk), length, count, qg_ref[0, chunk, 0], tile_of(0, chunk), weights.at[chunk]
        )
        totals[chunk] = jnp.broadcast_to(total, (PAIR, HEAD))
        share(0, chunk, a, lse)
        return 0

    def answer_chunk(a, _):
        chunk = chunk_at(a)
        grad, delta = answer(
            totals[chunk][:, :1], cotangent(0, chunk, base_of(chunk)),
            tile_of(0, chunk), tile_of(1, chunk), weights.at[chunk], dprobs,
        )
        grads[0, chunk] = grad
        share(1, chunk, a, delta)
        send_out(0, a)
        return 0

    def value_chunk(a):
        chunk = chunk_at(a)
        base = base_of(chunk)
        gv = jnp.zeros((PAIR, HEAD), jnp.float32)
        for d in range(3):
            prob = seen_again(
                d, base, length, kv_ref[0, chunk, 0], qg_ref[d, chunk, 0], stats[0, d, chunk, 0:1]
            )
            probs[chunk, d] = prob
            gv += dot(prob.astype(jnp.bfloat16), cotangent(d, chunk, base))
        grads[2, chunk] = gv.astype(jnp.bfloat16)
        send_out(2, a)

    def key_chunk(a, _):
        chunk = chunk_at(a)
        base = base_of(chunk)
        gk = jnp.zeros((PAIR, HEAD), jnp.float32)
        for d in range(3):
            dprob = dot_nt(kv_ref[0, chunk, 1], cotangent(d, chunk, base))
            ds = probs[chunk, d] * (dprob - stats[1, d, chunk, 0:1])
            gk += dot(ds.astype(jnp.bfloat16), qg_ref[d, chunk, 0])
        grads[1, chunk] = (gk * (1.0 / math.sqrt(HEAD))).astype(jnp.bfloat16)
        send_out(1, a)
        return 0

    lax.fori_loop(0, 2, weigh_chunk, 0)
    qg.hop(1, 2)
    lax.fori_loop(2, 3, weigh_chunk, 0)
    qg.hop(1, 3)
    settle(1)
    lax.fori_loop(0, 1, answer_chunk, 0)
    lax.fori_loop(3, 4, weigh_chunk, 0)
    lax.fori_loop(1, 4, answer_chunk, 0)
    shared(0)
    turned = (y >= NY - 2).astype(jnp.int32)
    for a in range(NX):
        qg.landed(a)
        value_chunk((a + turned) % NX)
    shared(1)
    lax.fori_loop(0, NX, key_chunk, 0)

    for n in range(3):
        own_out(n).wait()
        for i, (a, b) in enumerate(GROUP):
            if i:
                piece_out(n, a, b).wait()
    for kind in range(2):
        for d in (1, 2):
            for a in range(NX):
                stat_out(kind, d, a).wait_send()
    for copy in ended:
        copy.wait_send()


def backward(lengths, counts, lists, slots, queries, grads, keys, values, poolk, poolv):
    bf16, f32 = jnp.bfloat16, jnp.float32
    out = jax.ShapeDtypeStruct(queries.shape, bf16)
    dma = pltpu.SemaphoreType.DMA
    rows = (8, H * HEAD)
    return pl.pallas_call(
        kernel,
        name="backward",
        out_shape=(out,) * 3,
        in_specs=[SMEM] * 4 + [HBM] * 6,
        out_specs=(ANY,) * 3,
        scratch_shapes=[
            pltpu.VMEM((8, *rows), bf16),
            pltpu.VMEM((8, *rows), bf16),
            pltpu.VMEM((2, ZL, 4, *rows), bf16),
            pltpu.VMEM((2, ZL, 4, *rows), bf16),
            pltpu.VMEM((2, ZL, 4, *rows), bf16),
            pltpu.VMEM((ZL, 4, *rows), bf16),
            pltpu.VMEM((ZL, 4, *rows), bf16),
            pltpu.VMEM((2, 4, *rows), bf16),
            pltpu.VMEM((3, NX, 2, PAIR, HEAD), bf16),
            pltpu.VMEM((3, NX, 2, PAIR, HEAD), bf16),
            pltpu.VMEM((NY, 2, 4, H, 8, HEAD), bf16),
            pltpu.VMEM((4, 2, BLK, HEAD), bf16),
            pltpu.VMEM((NX, TILES, PAIR, PAIR), f32),
            pltpu.VMEM((TILES, PAIR, PAIR), f32),
            pltpu.VMEM((NX, PAIR, HEAD), f32),
            pltpu.VMEM((2, 3, NX, 8, PAIR), f32),
            pltpu.VMEM((3, NX, PAIR, HEAD), bf16),
            pltpu.VMEM((NX, 3, PAIR, PAIR), f32),
            dma((11,)),
            dma((4, 8)),
            dma((4, 8)),
            dma((2, 2)),
            dma((2, ZL)),
            dma((2, ZL)),
            dma((2, 8)),
            dma((2, 8)),
            dma((2, 2, NX)),
            dma((2, 2, NX)),
            dma((2, 2, UP)),
            dma((2, 2, UP)),
            dma((2, 2, NX)),
            dma((2, 2, NX)),
            dma((3, NX, NZ)),
            dma((3, NX, NZ)),
        ],
        compiler_params=pltpu.CompilerParams(
            collective_id=0, has_side_effects=True, vmem_limit_bytes=60 << 20
        ),
    )(lengths, counts, lists, slots, queries, grads, keys, values, poolk, poolv)


def finish_kernel(*refs):
    for n in range(3):
        refs[3 + n][...] = refs[n][...]


def finish(*parts):
    whole = pl.BlockSpec(memory_space=pltpu.VMEM)
    return pl.pallas_call(
        finish_kernel,
        name="finish",
        out_shape=tuple(jax.ShapeDtypeStruct(part.shape, part.dtype) for part in parts),
        in_specs=[whole] * 3,
        out_specs=(whole,) * 3,
    )(*parts)


def on_device(queries, keys, values, grad_out, mem_keys, mem_values, seq_lengths, mem_counts, block_lists, block_slots):
    parts = backward(
        seq_lengths, mem_counts, block_lists.T, block_slots, queries, grad_out, keys, values, mem_keys, mem_values
    )
    return finish(*parts)


def solution(mesh):
    rows = P("dp", "seq", None)
    return jax.shard_map(
        on_device,
        mesh=mesh,
        in_specs=(rows,) * 6 + (P(),) * 4,
        out_specs=(rows,) * 3,
        check_vma=False,
    )
```
